256 devices in a mesh: dp: 2 (over core), seq: 8 (over z), expert: 16 (over y, x).
Axes of the slice: x: 4, y: 4, z: 8, core: 2. Of those that a mesh axis runs over, the one named last changes fastest.
Arguments:
- tokens: bfloat16 [16384, 2048], P(('dp', 'seq')), may hold values from -6 to 6
- phi: bfloat16 [2048, 32], P(None, 'expert'), may hold values from -40 to 40
- w_in: bfloat16 [32, 2048, 8192], P('expert', None, ('dp', 'seq')), may hold values from -1 to 1
- w_out: bfloat16 [32, 8192, 2048], P('expert', ('dp', 'seq')), may hold values from -0.25 to 0.25
Outputs:
- mixed: bfloat16 [16384, 2048], P(('dp', 'seq', 'expert'))
The draws below stay inside these ranges and needn't reach their ends.
All inputs are finite; a program needn't handle non-finite values.
Results may differ from the reference program's by a relative error of at most 0.0068.
Values may be sent and summed in bfloat16 or wider, within the bound.
A program may use at most 64 MiB of HBM per device.

```python
import jax
import jax.numpy as jnp
from jax import lax

D = 2048
FF = 8192
EXPERTS = 32
LENGTH = 8192
CLIPS = 2
TOKENS = 16384


def drawn(key):
    base_key = jax.random.fold_in(key, 7)
    key_tok, key_phi = jax.random.split(base_key, 2)
    tokens = jnp.clip(jax.random.normal(key_tok, (TOKENS, D), jnp.float32), -5.0, 5.0)
    phi = jax.random.normal(key_phi, (D, EXPERTS), jnp.float32) * (2.0 / jnp.sqrt(jnp.float32(D)))
    return (tokens, phi)


def draw_tokens(key, part):
    return drawn(key)[0].astype(jnp.bfloat16)


def draw_phi(key, part):
    return drawn(key)[1].astype(jnp.bfloat16)


def levels(rng, dims, cuts, smallest, high):
    gain, own = 1.0, jax.random.fold_in(rng, 6)
    for dim, blocks in cuts:
        draws = jnp.exp(jax.random.uniform(jax.random.fold_in(own, dim), (blocks,), jnp.float32, smallest / len(cuts), high / len(cuts)))
        gain = gain * jnp.repeat(draws, dims[dim] // blocks).reshape([-1 if axis == dim else 1 for axis in range(len(dims))])
    return gain


def normal_values(stream_key, shape, scale, most, shards=(), dtype=jnp.bfloat16):
    drawn = jax.random.normal(stream_key, shape, jnp.float32) * scale
    if len(shards) > 0:
        drawn = levels(stream_key, shape, shards, -0.22, 0.18) * drawn
    return jnp.clip(drawn, min=-most, max=most).astype(dtype)


def setup_inputs(seed: int = 0) -> dict:
    arg_keys = jax.random.split(jax.random.key(seed), 5)
    return {
        "tokens": draw_tokens(jax.random.fold_in(arg_keys[4], 71), 0),
        "phi": draw_phi(jax.random.fold_in(arg_keys[4], 71), 0),
        "w_in": normal_values(arg_keys[2], (EXPERTS, D, FF), (D // 64) ** -0.5, 1.0, ((0, 16), (2, 16))),
        "w_out": normal_values(arg_keys[3], (EXPERTS, FF, D), (FF // 16) ** -0.5, 0.25, ((0, 16), (1, 16))),
    }


def expert_layer(packed):
    inputs, first, second = packed
    hidden = jax.nn.gelu(jnp.dot(inputs, first, preferred_element_type=jnp.float32), approximate=True).astype(jnp.bfloat16)
    return jnp.dot(hidden, second, preferred_element_type=jnp.float32).astype(jnp.bfloat16)


def reference(tokens, phi, w_in, w_out):
    clip_rows = tokens.reshape(CLIPS, LENGTH, D)
    logits = jnp.stack([lax.dot_general(phi, clip_rows[clip_index], (((0,), (1,)), ((), ())), preferred_element_type=jnp.float32) for clip_index in range(CLIPS)])
    slot_max = jnp.max(logits, axis=2, keepdims=True)
    spread = jnp.exp(logits - slot_max)
    spread_b = spread.astype(jnp.bfloat16)
    numerator = jnp.stack([jnp.dot(spread_b[clip_index], clip_rows[clip_index], preferred_element_type=jnp.float32) for clip_index in range(CLIPS)])
    denominator = jnp.sum(spread, axis=2)
    slot_in = (numerator / denominator[:, :, None]).astype(jnp.bfloat16)
    slot_out = lax.map(expert_layer, (jnp.transpose(slot_in, (1, 0, 2)), w_in, w_out))
    slot_out = jnp.transpose(slot_out, (1, 0, 2))
    row_max = jnp.max(logits, axis=1, keepdims=True)
    weight = jnp.exp(logits - row_max)
    weight_b = weight.astype(jnp.bfloat16)
    outputs = []
    for clip_index in range(CLIPS):
        summed = lax.dot_general(weight_b[clip_index], slot_out[clip_index], (((0,), (0,)), ((), ())), preferred_element_type=jnp.float32)
        totals = jnp.sum(weight[clip_index], axis=0)
        outputs.append((summed / totals[:, None]).astype(jnp.bfloat16))
    return jnp.concatenate(outputs, axis=0)
```

```python
import jax
import jax.numpy as jnp
from jax import lax
from jax.sharding import PartitionSpec as P


def on_device(tokens, phi, w_in, w_out):
    n_expert = lax.axis_size("expert")
    rows_out = tokens.shape[0] // n_expert
    phi_all = lax.all_gather(phi, "expert", axis=1, tiled=True)
    logits = lax.dot_general(
        phi, tokens, (((0,), (1,)), ((), ())), preferred_element_type=jnp.float32
    )
    slot_max = lax.pmax(jnp.max(logits, axis=1), "seq")
    spread = jnp.exp(logits - slot_max[:, None])
    numerator = jnp.dot(spread.astype(jnp.bfloat16), tokens, preferred_element_type=jnp.float32)
    denominator = jnp.sum(spread, axis=1)
    numer_seq, denom_seq = lax.psum((numerator, denominator), "seq")
    own_slots = (numer_seq / denom_seq[:, None]).astype(jnp.bfloat16)
    slot_in = lax.all_gather(own_slots[None], "dp", axis=0, tiled=True)
    hidden = jax.nn.gelu(
        jnp.einsum("ced,edf->cef", slot_in, w_in, preferred_element_type=jnp.float32),
        approximate=True,
    ).astype(jnp.bfloat16)
    partial_value = jnp.einsum("cef,efd->ced", hidden, w_out, preferred_element_type=jnp.float32)
    totals = lax.psum(partial_value, ("dp", "seq"))
    summed = lax.dynamic_index_in_dim(totals, lax.axis_index("dp"), 0, keepdims=False)
    slot_out = lax.all_gather(summed.astype(jnp.bfloat16), "expert", axis=0, tiled=True)
    rows = lax.dynamic_slice_in_dim(tokens, lax.axis_index("expert") * rows_out, rows_out, 0)
    row_logits = lax.dot_general(
        phi_all, rows, (((0,), (1,)), ((), ())), preferred_element_type=jnp.float32
    )
    row_max = jnp.max(row_logits, axis=0)
    combine_weights = jnp.exp(row_logits - row_max[None, :])
    mixed_numer = lax.dot_general(
        combine_weights.astype(jnp.bfloat16),
        slot_out,
        (((0,), (0,)), ((), ())),
        preferred_element_type=jnp.float32,
    )
    mixed_denom = jnp.sum(combine_weights, axis=0)
    return (mixed_numer / mixed_denom[:, None]).astype(jnp.bfloat16)


def solution(mesh):
    placed = (
        P(("dp", "seq"), None),
        P(None, "expert"),
        P("expert", None, ("dp", "seq")),
        P("expert", ("dp", "seq"), None),
    )
    return jax.shard_map(
        on_device,
        mesh=mesh,
        in_specs=placed,
        out_specs=P(("dp", "seq", "expert"), None),
        check_vma=False,
    )
```

```python
import functools

import jax
import jax.numpy as jnp
from jax import lax
from jax.experimental import pallas as pl
from jax.experimental.pallas import tpu as pltpu
from jax.sharding import PartitionSpec as P

MESH = pl.DeviceIdType.MESH
AXES = ("dp", "seq", "expert")


def _peer_coords(group, rank):
    coords = {a: lax.axis_index(a) for a in AXES}
    sizes = [lax.axis_size(a) for a in group]
    rest = rank
    for a, s in reversed(list(zip(group, sizes))):
        coords[a] = lax.rem(rest, s)
        rest = rest // s
    return tuple(coords[a] for a in AXES)


def _my_rank(group):
    rank = 0
    for a in group:
        rank = rank * lax.axis_size(a) + lax.axis_index(a)
    return rank


def _exchange_kernel(group, n, select, x_ref, o_ref, land, send_sem, recv_sem):
    me = _my_rank(group)
    barrier = pltpu.get_barrier_semaphore()
    for k in range(1, n):
        peer = _peer_coords(group, lax.rem(me + k, n))
        pl.semaphore_signal(barrier, inc=1, device_id=peer, device_id_type=MESH)
    pl.semaphore_wait(barrier, n - 1)

    def src_for(coords):
        if select is None:
            return x_ref
        return x_ref.at[coords[AXES.index(select)]]

    copies = []
    for k in range(1, n):
        peer = _peer_coords(group, lax.rem(me + k, n))
        copy = pltpu.make_async_remote_copy(
            src_ref=src_for(peer),
            dst_ref=land.at[me],
            send_sem=send_sem.at[k],
            recv_sem=recv_sem.at[k],
            device_id=peer,
            device_id_type=MESH,
        )
        copy.start()
        copies.append(copy)
    for copy in copies:
        copy.wait_send()
    for k in range(1, n):
        src_rank = lax.rem(me + n - k, n)
        pltpu.make_async_remote_copy(
            src_ref=src_for(_peer_coords(group, src_rank)),
            dst_ref=land.at[src_rank],
            send_sem=send_sem.at[k],
            recv_sem=recv_sem.at[k],
            device_id=_peer_coords(group, src_rank),
            device_id_type=MESH,
        ).wait_recv()
    o_ref[...] = land[...]
    own = src_for(_peer_coords(group, me))
    o_ref[me] = own[...]


def exchange(x, group, cid, select=None):
    n = 1
    for a in group:
        n *= lax.axis_size(a)
    block = x.shape if select is None else x.shape[1:]
    return pl.pallas_call(
        functools.partial(_exchange_kernel, group, n, select),
        out_shape=jax.ShapeDtypeStruct((n,) + block, x.dtype),
        in_specs=[pl.BlockSpec(memory_space=pltpu.VMEM)],
        out_specs=pl.BlockSpec(memory_space=pltpu.VMEM),
        scratch_shapes=[
            pltpu.VMEM((n,) + block, x.dtype),
            pltpu.SemaphoreType.DMA((n,)),
            pltpu.SemaphoreType.DMA((n,)),
        ],
        compiler_params=pltpu.CompilerParams(collective_id=cid, has_side_effects=True),
    )(x)


def on_device(tokens, phi, w_in, w_out):
    n_expert = lax.axis_size("expert")
    n_dp = lax.axis_size("dp")
    n_seq = lax.axis_size("seq")
    own_e = phi.shape[1]
    d = tokens.shape[1]
    rows_out = tokens.shape[0] // n_expert
    logits = lax.dot_general(
        phi, tokens, (((0,), (1,)), ((), ())), preferred_element_type=jnp.float32
    )
    local_max = jnp.broadcast_to(jnp.max(logits, axis=1)[:, None], (own_e, 128))
    slot_max = jnp.max(exchange(local_max, ("seq",), 0), axis=0)[:, 0]
    spread = jnp.exp(logits - slot_max[:, None])
    numerator = jnp.dot(spread.astype(jnp.bfloat16), tokens, preferred_element_type=jnp.float32)
    denominator = jnp.broadcast_to(jnp.sum(spread, axis=1)[:, None], (own_e, 128))
    stats = exchange(jnp.concatenate([numerator, denominator], axis=1), ("dp", "seq"), 1)
    stats = jnp.sum(stats.reshape(n_dp, n_seq, own_e, d + 128), axis=1)
    slot_in = (stats[:, :, :d] / stats[:, :, d:d + 1]).astype(jnp.bfloat16)
    hidden = jax.nn.gelu(
        jnp.einsum("ced,edf->cef", slot_in, w_in, preferred_element_type=jnp.float32),
        approximate=True,
    ).astype(jnp.bfloat16)
    partial_value = jnp.einsum("cef,efd->ced", hidden, w_out, preferred_element_type=jnp.float32)
    summed = jnp.sum(exchange(partial_value, ("dp", "seq"), 2, select="dp"), axis=0)
    packed = jnp.concatenate([phi.T, summed.astype(jnp.bfloat16)], axis=0)
    gathered = exchange(packed, ("expert",), 3)
    phi_all = gathered[:, :own_e].reshape(n_expert * own_e, d)
    slot_out = gathered[:, own_e:].reshape(n_expert * own_e, d)
    rows = lax.dynamic_slice_in_dim(tokens, lax.axis_index("expert") * rows_out, rows_out, 0)
    row_logits = lax.dot_general(
        phi_all, rows, (((1,), (1,)), ((), ())), preferred_element_type=jnp.float32
    )
    row_max = jnp.max(row_logits, axis=0)
    combine_weights = jnp.exp(row_logits - row_max[None, :])
    mixed_numer = lax.dot_general(
        combine_weights.astype(jnp.bfloat16),
        slot_out,
        (((0,), (0,)), ((), ())),
        preferred_element_type=jnp.float32,
    )
    mixed_denom = jnp.sum(combine_weights, axis=0)
    return (mixed_numer / mixed_denom[:, None]).astype(jnp.bfloat16)


def solution(mesh):
    placed = (
        P(("dp", "seq"), None),
        P(None, "expert"),
        P("expert", None, ("dp", "seq")),
        P("expert", ("dp", "seq"), None),
    )
    return jax.shard_map(
        on_device,
        mesh=mesh,
        in_specs=placed,
        out_specs=P(("dp", "seq", "expert"), None),
        check_vma=False,
    )
```

```python
import functools

import jax
import jax.numpy as jnp
from jax import lax
from jax.experimental import pallas as pl
from jax.experimental.pallas import tpu as pltpu
from jax.sharding import PartitionSpec as P

MESH = pl.DeviceIdType.MESH
AXES = ("dp", "seq", "expert")


def _peer_coords(group, rank):
    coords = {a: lax.axis_index(a) for a in AXES}
    sizes = [lax.axis_size(a) for a in group]
    rest = rank
    for a, s in reversed(list(zip(group, sizes))):
        coords[a] = lax.rem(rest, s)
        rest = rest // s
    return tuple(coords[a] for a in AXES)


def _my_rank(group):
    rank = 0
    for a in group:
        rank = rank * lax.axis_size(a) + lax.axis_index(a)
    return rank


def _exchange_kernel(group, n, select, x_ref, o_ref, land, send_sem, recv_sem):
    me = _my_rank(group)
    barrier = pltpu.get_barrier_semaphore()
    for k in range(1, n):
        peer = _peer_coords(group, lax.rem(me + k, n))
        pl.semaphore_signal(barrier, inc=1, device_id=peer, device_id_type=MESH)
    pl.semaphore_wait(barrier, n - 1)

    def src_for(coords):
        if select is None:
            return x_ref
        return x_ref.at[coords[AXES.index(select)]]

    copies = []
    for k in range(1, n):
        peer = _peer_coords(group, lax.rem(me + k, n))
        copy = pltpu.make_async_remote_copy(
            src_ref=src_for(peer),
            dst_ref=land.at[me],
            send_sem=send_sem.at[k],
            recv_sem=recv_sem.at[k],
            device_id=peer,
            device_id_type=MESH,
        )
        copy.start()
        copies.append(copy)
    for copy in copies:
        copy.wait_send()
    for k in range(1, n):
        src_rank = lax.rem(me + n - k, n)
        pltpu.make_async_remote_copy(
            src_ref=src_for(_peer_coords(group, src_rank)),
            dst_ref=land.at[src_rank],
            send_sem=send_sem.at[k],
            recv_sem=recv_sem.at[k],
            device_id=_peer_coords(group, src_rank),
            device_id_type=MESH,
        ).wait_recv()
    o_ref[...] = land[...]
    own = src_for(_peer_coords(group, me))
    o_ref[me] = own[...]


def exchange(x, group, cid, select=None):
    n = 1
    for a in group:
        n *= lax.axis_size(a)
    block = x.shape if select is None else x.shape[1:]
    return pl.pallas_call(
        functools.partial(_exchange_kernel, group, n, select),
        out_shape=jax.ShapeDtypeStruct((n,) + block, x.dtype),
        in_specs=[pl.BlockSpec(memory_space=pltpu.VMEM)],
        out_specs=pl.BlockSpec(memory_space=pltpu.VMEM),
        scratch_shapes=[
            pltpu.VMEM((n,) + block, x.dtype),
            pltpu.SemaphoreType.DMA((n,)),
            pltpu.SemaphoreType.DMA((n,)),
        ],
        compiler_params=pltpu.CompilerParams(collective_id=cid, has_side_effects=True),
    )(x)


def _reduce_then_gather_kernel(g1, n1, g2, n2, x_ref, phi_ref, o_ref, land1, send2, land2, s1, r1, s2, r2):
    me1, me2 = _my_rank(g1), _my_rank(g2)
    barrier = pltpu.get_barrier_semaphore()
    for group, me, n in ((g1, me1, n1), (g2, me2, n2)):
        for k in range(1, n):
            peer = _peer_coords(group, lax.rem(me + k, n))
            pl.semaphore_signal(barrier, inc=1, device_id=peer, device_id_type=MESH)
    pl.semaphore_wait(barrier, n1 - 1 + n2 - 1)

    def run(group, me, n, src_for, land, ssem, rsem):
        copies = []
        for k in range(1, n):
            peer = _peer_coords(group, lax.rem(me + k, n))
            copy = pltpu.make_async_remote_copy(
                src_ref=src_for(peer), dst_ref=land.at[me], send_sem=ssem.at[k],
                recv_sem=rsem.at[k], device_id=peer, device_id_type=MESH,
            )
            copy.start()
            copies.append(copy)
        for copy in copies:
            copy.wait_send()
        for k in range(1, n):
            src_rank = lax.rem(me + n - k, n)
            peer = _peer_coords(group, src_rank)
            pltpu.make_async_remote_copy(
                src_ref=src_for(peer), dst_ref=land.at[src_rank], send_sem=ssem.at[k],
                recv_sem=rsem.at[k], device_id=peer, device_id_type=MESH,
            ).wait_recv()

    dp_pos = AXES.index("dp")
    run(g1, me1, n1, lambda c: x_ref.at[c[dp_pos]], land1, s1, r1)
    land1[me1] = x_ref[lax.axis_index("dp")]
    total = jnp.sum(land1[...], axis=0)
    send2[...] = jnp.concatenate([phi_ref[...], total.astype(send2.dtype)], axis=0)
    run(g2, me2, n2, lambda c: send2, land2, s2, r2)
    land2[me2] = send2[...]
    o_ref[...] = land2[...]


def reduce_then_gather(x, phi_t, cid):
    g1, g2 = ("dp", "seq"), ("expert",)
    n1 = lax.axis_size("dp") * lax.axis_size("seq")
    n2 = lax.axis_size("expert")
    rows, d = x.shape[1], x.shape[2]
    packed = (phi_t.shape[0] + rows, d)
    return pl.pallas_call(
        functools.partial(_reduce_then_gather_kernel, g1, n1, g2, n2),
        out_shape=jax.ShapeDtypeStruct((n2,) + packed, phi_t.dtype),
        in_specs=[pl.BlockSpec(memory_space=pltpu.VMEM)] * 2,
        out_specs=pl.BlockSpec(memory_space=pltpu.VMEM),
        scratch_shapes=[
            pltpu.VMEM((n1, rows, d), x.dtype),
            pltpu.VMEM(packed, phi_t.dtype),
            pltpu.VMEM((n2,) + packed, phi_t.dtype),
            pltpu.SemaphoreType.DMA((n1,)),
            pltpu.SemaphoreType.DMA((n1,)),
            pltpu.SemaphoreType.DMA((n2,)),
            pltpu.SemaphoreType.DMA((n2,)),
        ],
        compiler_params=pltpu.CompilerParams(collective_id=cid, has_side_effects=True),
    )(x, phi_t)


def on_device(tokens, phi, w_in, w_out):
    n_expert = lax.axis_size("expert")
    n_dp = lax.axis_size("dp")
    n_seq = lax.axis_size("seq")
    own_e = phi.shape[1]
    d = tokens.shape[1]
    rows_out = tokens.shape[0] // n_expert
    logits = lax.dot_general(
        phi, tokens, (((0,), (1,)), ((), ())), preferred_element_type=jnp.float32
    )
    local_max = jnp.max(logits, axis=1)
    spread = jnp.exp(logits - local_max[:, None])
    numerator = jnp.dot(spread.astype(jnp.bfloat16), tokens, preferred_element_type=jnp.float32)
    denominator = jnp.sum(spread, axis=1)
    side = jnp.concatenate(
        [jnp.broadcast_to(denominator[:, None], (own_e, 128)),
         jnp.broadcast_to(local_max[:, None], (own_e, 128))], axis=1)
    stats = exchange(jnp.concatenate([numerator, side], axis=1), ("dp", "seq"), 1)
    stats = stats.reshape(n_dp, n_seq, own_e, d + 256)
    part_max = stats[:, :, :, d + 128]
    rescale = jnp.exp(part_max - jnp.max(part_max, axis=1, keepdims=True))
    numer = jnp.sum(stats[:, :, :, :d] * rescale[..., None], axis=1)
    denom = jnp.sum(stats[:, :, :, d] * rescale, axis=1)
    slot_in = (numer / denom[..., None]).astype(jnp.bfloat16)
    hidden = jax.nn.gelu(
        jnp.einsum("ced,edf->cef", slot_in, w_in, preferred_element_type=jnp.float32),
        approximate=True,
    ).astype(jnp.bfloat16)
    partial_value = jnp.einsum("cef,efd->ced", hidden, w_out, preferred_element_type=jnp.float32)
    gathered = reduce_then_gather(partial_value, phi.T, 2)
    phi_all = gathered[:, :own_e].reshape(n_expert * own_e, d)
    slot_out = gathered[:, own_e:].reshape(n_expert * own_e, d)
    rows = lax.dynamic_slice_in_dim(tokens, lax.axis_index("expert") * rows_out, rows_out, 0)
    row_logits = lax.dot_general(
        phi_all, rows, (((1,), (1,)), ((), ())), preferred_element_type=jnp.float32
    )
    row_max = jnp.max(row_logits, axis=0)
    combine_weights = jnp.exp(row_logits - row_max[None, :])
    mixed_numer = lax.dot_general(
        combine_weights.astype(jnp.bfloat16),
        slot_out,
        (((0,), (0,)), ((), ())),
        preferred_element_type=jnp.float32,
    )
    mixed_denom = jnp.sum(combine_weights, axis=0)
    return (mixed_numer / mixed_denom[:, None]).astype(jnp.bfloat16)


def solution(mesh):
    placed = (
        P(("dp", "seq"), None),
        P(None, "expert"),
        P("expert", None, ("dp", "seq")),
        P("expert", ("dp", "seq"), None),
    )
    return jax.shard_map(
        on_device,
        mesh=mesh,
        in_specs=placed,
        out_specs=P(("dp", "seq", "expert"), None),
        check_vma=False,
    )
```

```python
import functools

import jax
import jax.numpy as jnp
from jax import lax
from jax.experimental import pallas as pl
from jax.experimental.pallas import tpu as pltpu
from jax.sharding import PartitionSpec as P

MESH = pl.DeviceIdType.MESH
AXES = ("dp", "seq", "expert")


def _peer_coords(group, rank):
    coords = {a: lax.axis_index(a) for a in AXES}
    sizes = [lax.axis_size(a) for a in group]
    rest = rank
    for a, s in reversed(list(zip(group, sizes))):
        coords[a] = lax.rem(rest, s)
        rest = rest // s
    return tuple(coords[a] for a in AXES)


def _my_rank(group):
    rank = 0
    for a in group:
        rank = rank * lax.axis_size(a) + lax.axis_index(a)
    return rank


def _exchange_kernel(group, n, select, x_ref, o_ref, land, send_sem, recv_sem):
    me = _my_rank(group)
    barrier = pltpu.get_barrier_semaphore()
    for k in range(1, n):
        peer = _peer_coords(group, lax.rem(me + k, n))
        pl.semaphore_signal(barrier, inc=1, device_id=peer, device_id_type=MESH)
    pl.semaphore_wait(barrier, n - 1)

    def src_for(coords):
        if select is None:
            return x_ref
        return x_ref.at[coords[AXES.index(select)]]

    copies = []
    for k in range(1, n):
        peer = _peer_coords(group, lax.rem(me + k, n))
        copy = pltpu.make_async_remote_copy(
            src_ref=src_for(peer),
            dst_ref=land.at[me],
            send_sem=send_sem.at[k],
            recv_sem=recv_sem.at[k],
            device_id=peer,
            device_id_type=MESH,
        )
        copy.start()
        copies.append(copy)
    for copy in copies:
        copy.wait_send()
    for k in range(1, n):
        src_rank = lax.rem(me + n - k, n)
        pltpu.make_async_remote_copy(
            src_ref=src_for(_peer_coords(group, src_rank)),
            dst_ref=land.at[src_rank],
            send_sem=send_sem.at[k],
            recv_sem=recv_sem.at[k],
            device_id=_peer_coords(group, src_rank),
            device_id_type=MESH,
        ).wait_recv()
    o_ref[...] = land[...]
    own = src_for(_peer_coords(group, me))
    o_ref[me] = own[...]


def exchange(x, group, cid, select=None):
    n = 1
    for a in group:
        n *= lax.axis_size(a)
    block = x.shape if select is None else x.shape[1:]
    return pl.pallas_call(
        functools.partial(_exchange_kernel, group, n, select),
        out_shape=jax.ShapeDtypeStruct((n,) + block, x.dtype),
        in_specs=[pl.BlockSpec(memory_space=pltpu.VMEM)],
        out_specs=pl.BlockSpec(memory_space=pltpu.VMEM),
        scratch_shapes=[
            pltpu.VMEM((n,) + block, x.dtype),
            pltpu.SemaphoreType.DMA((n,)),
            pltpu.SemaphoreType.DMA((n,)),
        ],
        compiler_params=pltpu.CompilerParams(collective_id=cid, has_side_effects=True),
    )(x)


def _send_all(group, me, n, src_for, land, ssem, rsem):
    copies = []
    for k in range(1, n):
        peer = _peer_coords(group, lax.rem(me + k, n))
        copy = pltpu.make_async_remote_copy(
            src_ref=src_for(peer), dst_ref=land.at[me], send_sem=ssem.at[k],
            recv_sem=rsem.at[k], device_id=peer, device_id_type=MESH,
        )
        copy.start()
        copies.append(copy)
    return copies


def _wait_all(group, me, n, src_for, land, ssem, rsem, copies):
    for copy in copies:
        copy.wait_send()
    for k in range(1, n):
        src_rank = lax.rem(me + n - k, n)
        peer = _peer_coords(group, src_rank)
        pltpu.make_async_remote_copy(
            src_ref=src_for(peer), dst_ref=land.at[src_rank], send_sem=ssem.at[k],
            recv_sem=rsem.at[k], device_id=peer, device_id_type=MESH,
        ).wait_recv()


def _gelu(v):
    return 0.5 * v * (1.0 + jnp.tanh(0.7978845608028654 * (v + 0.044715 * v * v * v)))


def _slots_kernel(n_dp, n_seq, n_ex, num_ref, side_ref, phi_ref, w_in_hbm, w_out_hbm,
                  phi_out, so_out, w_in_v, w_out_v, w_sem, num_land, side_land, phi_land,
                  slot_in, part_src, part_land, so_src, so_land, sems):
    g1, g2 = ("dp", "seq"), ("expert",)
    n1 = n_dp * n_seq
    me1, me2 = _my_rank(g1), _my_rank(g2)
    my_dp = lax.axis_index("dp")
    w_in_copy = pltpu.make_async_copy(w_in_hbm, w_in_v, w_sem.at[0])
    w_out_copy = pltpu.make_async_copy(w_out_hbm, w_out_v, w_sem.at[1])
    w_in_copy.start()
    w_out_copy.start()

    barrier = pltpu.get_barrier_semaphore()
    for group, me, n in ((g1, me1, n1), (g2, me2, n_ex)):
        for k in range(1, n):
            peer = _peer_coords(group, lax.rem(me + k, n))
            pl.semaphore_signal(barrier, inc=1, device_id=peer, device_id_type=MESH)
    pl.semaphore_wait(barrier, n1 - 1 + n_ex - 1)

    stage_a = [
        (g1, me1, n1, lambda c: num_ref, num_land, sems.at[0], sems.at[1]),
        (g1, me1, n1, lambda c: side_ref, side_land, sems.at[2], sems.at[3]),
        (g2, me2, n_ex, lambda c: phi_ref, phi_land, sems.at[4], sems.at[5]),
    ]
    started = [_send_all(*args) for args in stage_a]
    for args, copies in zip(stage_a, started):
        _wait_all(*args, copies)
    num_land[me1] = num_ref[...]
    side_land[me1] = side_ref[...]
    phi_land[me2] = phi_ref[...]
    phi_out[...] = phi_land[...]

    own_e = num_ref.shape[0]
    for c in range(n_dp):
        rows = pl.ds(c * n_seq, n_seq)
        side = side_land[rows]
        part_max = side[:, :, 128:256]
        scale = jnp.exp(part_max - jnp.max(part_max, axis=0, keepdims=True))
        denom = jnp.sum(side[:, :, 0:128] * scale, axis=0)
        numer = jnp.sum(num_land[rows] * scale[:, :, 0:1], axis=0)
        value = (numer / denom[:, 0:1]).astype(jnp.bfloat16).astype(jnp.float32)
        for e in range(own_e):
            slot_in[e, pl.ds(c, 1), :] = value[e:e + 1, :]

    w_in_copy.wait()
    w_out_copy.wait()
    for e in range(own_e):
        hidden = jnp.dot(slot_in[e].astype(jnp.bfloat16), w_in_v[e], preferred_element_type=jnp.float32)
        hidden = _gelu(hidden).astype(jnp.bfloat16)
        part = jnp.dot(hidden, w_out_v[e], preferred_element_type=jnp.float32)
        for c in range(n_dp):
            part_src[c, pl.ds(e, 1), :] = part[c:c + 1, :]

    dp_pos = AXES.index("dp")
    stage_b = (g1, me1, n1, lambda c: part_src.at[c[dp_pos]], part_land, sems.at[6], sems.at[7])
    _wait_all(*stage_b, _send_all(*stage_b))
    part_land[me1] = part_src[my_dp]
    so_src[...] = jnp.sum(part_land[...], axis=0).astype(so_src.dtype)

    stage_c = (g2, me2, n_ex, lambda c: so_src, so_land, sems.at[8], sems.at[9])
    _wait_all(*stage_c, _send_all(*stage_c))
    so_land[me2] = so_src[...]
    so_out[...] = so_land[...]


def expert_slots(num, side, phi_t, w_in, w_out, cid):
    n_dp, n_seq, n_ex = (lax.axis_size(a) for a in AXES)
    n1 = n_dp * n_seq
    own_e, d = num.shape
    vmem = pl.BlockSpec(memory_space=pltpu.VMEM)
    anywhere = pl.BlockSpec(memory_space=pl.ANY)
    gathered = jax.ShapeDtypeStruct((n_ex, own_e, d), jnp.bfloat16)
    return pl.pallas_call(
        functools.partial(_slots_kernel, n_dp, n_seq, n_ex),
        out_shape=(gathered, gathered),
        in_specs=[vmem, vmem, vmem, anywhere, anywhere],
        out_specs=(vmem, vmem),
        scratch_shapes=[
            pltpu.VMEM(w_in.shape, w_in.dtype),
            pltpu.VMEM(w_out.shape, w_out.dtype),
            pltpu.SemaphoreType.DMA((2,)),
            pltpu.VMEM((n1, own_e, d), jnp.float32),
            pltpu.VMEM((n1,) + side.shape, jnp.float32),
            pltpu.VMEM((n_ex, own_e, d), jnp.bfloat16),
            pltpu.VMEM((own_e, n_dp, d), jnp.float32),
            pltpu.VMEM((n_dp, own_e, d), jnp.float32),
            pltpu.VMEM((n1, own_e, d), jnp.float32),
            pltpu.VMEM((own_e, d), jnp.bfloat16),
            pltpu.VMEM((n_ex, own_e, d), jnp.bfloat16),
            pltpu.SemaphoreType.DMA((10, max(n1, n_ex))),
        ],
        compiler_params=pltpu.CompilerParams(
            collective_id=cid, has_side_effects=True, vmem_limit_bytes=48 * 1024 * 1024
        ),
    )(num, side, phi_t, w_in, w_out)

def on_device(tokens, phi, w_in, w_out):
    n_expert = lax.axis_size("expert")
    n_dp = lax.axis_size("dp")
    n_seq = lax.axis_size("seq")
    own_e = phi.shape[1]
    d = tokens.shape[1]
    rows_out = tokens.shape[0] // n_expert
    logits = lax.dot_general(
        phi, tokens, (((0,), (1,)), ((), ())), preferred_element_type=jnp.float32
    )
    local_max = jnp.max(logits, axis=1)
    spread = jnp.exp(logits - local_max[:, None])
    numerator = jnp.dot(spread.astype(jnp.bfloat16), tokens, preferred_element_type=jnp.float32)
    denominator = jnp.sum(spread, axis=1)
    side = jnp.concatenate(
        [jnp.broadcast_to(denominator[:, None], (own_e, 128)),
         jnp.broadcast_to(local_max[:, None], (own_e, 128))], axis=1)
    phi_g, slot_g = expert_slots(numerator, side, phi.T, w_in, w_out, 1)
    phi_all = phi_g.reshape(n_expert * own_e, d)
    slot_out = slot_g.reshape(n_expert * own_e, d)
    rows = lax.dynamic_slice_in_dim(tokens, lax.axis_index("expert") * rows_out, rows_out, 0)
    row_logits = lax.dot_general(
        phi_all, rows, (((1,), (1,)), ((), ())), preferred_element_type=jnp.float32
    )
    row_max = jnp.max(row_logits, axis=0)
    combine_weights = jnp.exp(row_logits - row_max[None, :])
    mixed_numer = lax.dot_general(
        combine_weights.astype(jnp.bfloat16),
        slot_out,
        (((0,), (0,)), ((), ())),
        preferred_element_type=jnp.float32,
    )
    mixed_denom = jnp.sum(combine_weights, axis=0)
    return (mixed_numer / mixed_denom[:, None]).astype(jnp.bfloat16)


def solution(mesh):
    placed = (
        P(("dp", "seq"), None),
        P(None, "expert"),
        P("expert", None, ("dp", "seq")),
        P("expert", ("dp", "seq"), None),
    )
    return jax.shard_map(
        on_device,
        mesh=mesh,
        in_specs=placed,
        out_specs=P(("dp", "seq", "expert"), None),
        check_vma=False,
    )
```

```python
import functools

import jax
import jax.numpy as jnp
from jax import lax
from jax.experimental import pallas as pl
from jax.experimental.pallas import tpu as pltpu
from jax.sharding import PartitionSpec as P

MESH = pl.DeviceIdType.MESH
AXES = ("dp", "seq", "expert")


def _peer_coords(group, rank):
    coords = {a: lax.axis_index(a) for a in AXES}
    sizes = [lax.axis_size(a) for a in group]
    rest = rank
    for a, s in reversed(list(zip(group, sizes))):
        coords[a] = lax.rem(rest, s)
        rest = rest // s
    return tuple(coords[a] for a in AXES)


def _my_rank(group):
    rank = 0
    for a in group:
        rank = rank * lax.axis_size(a) + lax.axis_index(a)
    return rank


def _exchange_kernel(group, n, select, x_ref, o_ref, land, send_sem, recv_sem):
    me = _my_rank(group)
    barrier = pltpu.get_barrier_semaphore()
    for k in range(1, n):
        peer = _peer_coords(group, lax.rem(me + k, n))
        pl.semaphore_signal(barrier, inc=1, device_id=peer, device_id_type=MESH)
    pl.semaphore_wait(barrier, n - 1)

    def src_for(coords):
        if select is None:
            return x_ref
        return x_ref.at[coords[AXES.index(select)]]

    copies = []
    for k in range(1, n):
        peer = _peer_coords(group, lax.rem(me + k, n))
        copy = pltpu.make_async_remote_copy(
            src_ref=src_for(peer),
            dst_ref=land.at[me],
            send_sem=send_sem.at[k],
            recv_sem=recv_sem.at[k],
            device_id=peer,
            device_id_type=MESH,
        )
        copy.start()
        copies.append(copy)
    for copy in copies:
        copy.wait_send()
    for k in range(1, n):
        src_rank = lax.rem(me + n - k, n)
        pltpu.make_async_remote_copy(
            src_ref=src_for(_peer_coords(group, src_rank)),
            dst_ref=land.at[src_rank],
            send_sem=send_sem.at[k],
            recv_sem=recv_sem.at[k],
            device_id=_peer_coords(group, src_rank),
            device_id_type=MESH,
        ).wait_recv()
    o_ref[...] = land[...]
    own = src_for(_peer_coords(group, me))
    o_ref[me] = own[...]


def exchange(x, group, cid, select=None):
    n = 1
    for a in group:
        n *= lax.axis_size(a)
    block = x.shape if select is None else x.shape[1:]
    return pl.pallas_call(
        functools.partial(_exchange_kernel, group, n, select),
        out_shape=jax.ShapeDtypeStruct((n,) + block, x.dtype),
        in_specs=[pl.BlockSpec(memory_space=pltpu.VMEM)],
        out_specs=pl.BlockSpec(memory_space=pltpu.VMEM),
        scratch_shapes=[
            pltpu.VMEM((n,) + block, x.dtype),
            pltpu.SemaphoreType.DMA((n,)),
            pltpu.SemaphoreType.DMA((n,)),
        ],
        compiler_params=pltpu.CompilerParams(collective_id=cid, has_side_effects=True),
    )(x)


def _send_all(group, me, n, src_for, land, ssem, rsem):
    copies = []
    for k in range(1, n):
        peer = _peer_coords(group, lax.rem(me + k, n))
        copy = pltpu.make_async_remote_copy(
            src_ref=src_for(peer), dst_ref=land.at[me], send_sem=ssem.at[k],
            recv_sem=rsem.at[k], device_id=peer, device_id_type=MESH,
        )
        copy.start()
        copies.append(copy)
    return copies


def _wait_all(group, me, n, src_for, land, ssem, rsem, copies):
    for copy in copies:
        copy.wait_send()
    for k in range(1, n):
        src_rank = lax.rem(me + n - k, n)
        peer = _peer_coords(group, src_rank)
        pltpu.make_async_remote_copy(
            src_ref=src_for(peer), dst_ref=land.at[src_rank], send_sem=ssem.at[k],
            recv_sem=rsem.at[k], device_id=peer, device_id_type=MESH,
        ).wait_recv()


def _gelu(v):
    return 0.5 * v * (1.0 + jnp.tanh(0.7978845608028654 * (v + 0.044715 * v * v * v)))


def _slots_kernel(n_dp, n_seq, n_ex, tok_hbm, phi_ref, w_in_hbm, w_out_hbm,
                  phi_out, so_out, tok_v, num_ref, side_ref, w_in_v, w_out_v, w_sem, num_land,
                  side_land, phi_land, slot_in, part_src, part_land, so_src, so_land, sems):
    g1, g2 = ("dp", "seq"), ("expert",)
    n1 = n_dp * n_seq
    me1, me2 = _my_rank(g1), _my_rank(g2)
    my_dp = lax.axis_index("dp")
    tok_copy = pltpu.make_async_copy(tok_hbm, tok_v, w_sem.at[2])
    tok_copy.start()
    w_in_copy = pltpu.make_async_copy(w_in_hbm, w_in_v, w_sem.at[0])
    w_out_copy = pltpu.make_async_copy(w_out_hbm, w_out_v, w_sem.at[1])
    w_in_copy.start()
    w_out_copy.start()

    barrier = pltpu.get_barrier_semaphore()
    for group, me, n in ((g1, me1, n1), (g2, me2, n_ex)):
        for k in range(1, n):
            peer = _peer_coords(group, lax.rem(me + k, n))
            pl.semaphore_signal(barrier, inc=1, device_id=peer, device_id_type=MESH)

    tok_copy.wait()
    logits = lax.dot_general(
        phi_ref[...], tok_v[...], (((1,), (1,)), ((), ())), preferred_element_type=jnp.float32
    )
    local_max = jnp.max(logits, axis=1, keepdims=True)
    spread = jnp.exp(logits - local_max)
    denominator = jnp.sum(spread, axis=1, keepdims=True)
    num_ref[...] = jnp.dot(spread.astype(jnp.bfloat16), tok_v[...], preferred_element_type=jnp.float32)
    side_ref[:, 0:128] = jnp.broadcast_to(denominator, (denominator.shape[0], 128))
    side_ref[:, 128:256] = jnp.broadcast_to(local_max, (local_max.shape[0], 128))
    pl.semaphore_wait(barrier, n1 - 1 + n_ex - 1)

    stage_a = [
        (g1, me1, n1, lambda c: num_ref, num_land, sems.at[0], sems.at[1]),
        (g1, me1, n1, lambda c: side_ref, side_land, sems.at[2], sems.at[3]),
        (g2, me2, n_ex, lambda c: phi_ref, phi_land, sems.at[4], sems.at[5]),
    ]
    started = [_send_all(*args) for args in stage_a]
    for args, copies in zip(stage_a, started):
        _wait_all(*args, copies)
    num_land[me1] = num_ref[...]
    side_land[me1] = side_ref[...]
    phi_land[me2] = phi_ref[...]
    phi_out[...] = phi_land[...]

    own_e = num_ref.shape[0]
    for c in range(n_dp):
        rows = pl.ds(c * n_seq, n_seq)
        side = side_land[rows]
        part_max = side[:, :, 128:256]
        scale = jnp.exp(part_max - jnp.max(part_max, axis=0, keepdims=True))
        denom = jnp.sum(side[:, :, 0:128] * scale, axis=0)
        numer = jnp.sum(num_land[rows] * scale[:, :, 0:1], axis=0)
        value = (numer / denom[:, 0:1]).astype(jnp.bfloat16).astype(jnp.float32)
        for e in range(own_e):
            slot_in[e, pl.ds(c, 1), :] = value[e:e + 1, :]

    w_in_copy.wait()
    w_out_copy.wait()
    for e in range(own_e):
        hidden = jnp.dot(slot_in[e].astype(jnp.bfloat16), w_in_v[e], preferred_element_type=jnp.float32)
        hidden = _gelu(hidden).astype(jnp.bfloat16)
        part = jnp.dot(hidden, w_out_v[e], preferred_element_type=jnp.float32)
        for c in range(n_dp):
            part_src[c, pl.ds(e, 1), :] = part[c:c + 1, :]

    dp_pos = AXES.index("dp")
    stage_b = (g1, me1, n1, lambda c: part_src.at[c[dp_pos]], part_land, sems.at[6], sems.at[7])
    _wait_all(*stage_b, _send_all(*stage_b))
    part_land[me1] = part_src[my_dp]
    so_src[...] = jnp.sum(part_land[...], axis=0).astype(so_src.dtype)

    stage_c = (g2, me2, n_ex, lambda c: so_src, so_land, sems.at[8], sems.at[9])
    _wait_all(*stage_c, _send_all(*stage_c))
    so_land[me2] = so_src[...]
    so_out[...] = so_land[...]


def expert_slots(tokens, phi_t, w_in, w_out, cid):
    n_dp, n_seq, n_ex = (lax.axis_size(a) for a in AXES)
    n1 = n_dp * n_seq
    own_e, d = phi_t.shape
    vmem = pl.BlockSpec(memory_space=pltpu.VMEM)
    anywhere = pl.BlockSpec(memory_space=pl.ANY)
    gathered = jax.ShapeDtypeStruct((n_ex, own_e, d), jnp.bfloat16)
    return pl.pallas_call(
        functools.partial(_slots_kernel, n_dp, n_seq, n_ex),
        out_shape=(gathered, gathered),
        in_specs=[anywhere, vmem, anywhere, anywhere],
        out_specs=(vmem, vmem),
        scratch_shapes=[
            pltpu.VMEM(tokens.shape, tokens.dtype),
            pltpu.VMEM((own_e, d), jnp.float32),
            pltpu.VMEM((own_e, 256), jnp.float32),
            pltpu.VMEM(w_in.shape, w_in.dtype),
            pltpu.VMEM(w_out.shape, w_out.dtype),
            pltpu.SemaphoreType.DMA((3,)),
            pltpu.VMEM((n1, own_e, d), jnp.float32),
            pltpu.VMEM((n1, own_e, 256), jnp.float32),
            pltpu.VMEM((n_ex, own_e, d), jnp.bfloat16),
            pltpu.VMEM((own_e, n_dp, d), jnp.float32),
            pltpu.VMEM((n_dp, own_e, d), jnp.float32),
            pltpu.VMEM((n1, own_e, d), jnp.float32),
            pltpu.VMEM((own_e, d), jnp.bfloat16),
            pltpu.VMEM((n_ex, own_e, d), jnp.bfloat16),
            pltpu.SemaphoreType.DMA((10, max(n1, n_ex))),
        ],
        compiler_params=pltpu.CompilerParams(
            collective_id=cid, has_side_effects=True, vmem_limit_bytes=48 * 1024 * 1024
        ),
    )(tokens, phi_t, w_in, w_out)

def on_device(tokens, phi, w_in, w_out):
    n_expert = lax.axis_size("expert")
    n_dp = lax.axis_size("dp")
    n_seq = lax.axis_size("seq")
    own_e = phi.shape[1]
    d = tokens.shape[1]
    rows_out = tokens.shape[0] // n_expert
    phi_g, slot_g = expert_slots(tokens, phi.T, w_in, w_out, 1)
    phi_all = phi_g.reshape(n_expert * own_e, d)
    slot_out = slot_g.reshape(n_expert * own_e, d)
    rows = lax.dynamic_slice_in_dim(tokens, lax.axis_index("expert") * rows_out, rows_out, 0)
    row_logits = lax.dot_general(
        phi_all, rows, (((1,), (1,)), ((), ())), preferred_element_type=jnp.float32
    )
    row_max = jnp.max(row_logits, axis=0)
    combine_weights = jnp.exp(row_logits - row_max[None, :])
    mixed_numer = lax.dot_general(
        combine_weights.astype(jnp.bfloat16),
        slot_out,
        (((0,), (0,)), ((), ())),
        preferred_element_type=jnp.float32,
    )
    mixed_denom = jnp.sum(combine_weights, axis=0)
    return (mixed_numer / mixed_denom[:, None]).astype(jnp.bfloat16)


def solution(mesh):
    placed = (
        P(("dp", "seq"), None),
        P(None, "expert"),
        P("expert", None, ("dp", "seq")),
        P("expert", ("dp", "seq"), None),
    )
    return jax.shard_map(
        on_device,
        mesh=mesh,
        in_specs=placed,
        out_specs=P(("dp", "seq", "expert"), None),
        check_vma=False,
    )
```

```python
import functools

import jax
import jax.numpy as jnp
from jax import lax
from jax.experimental import pallas as pl
from jax.experimental.pallas import tpu as pltpu
from jax.sharding import PartitionSpec as P

MESH = pl.DeviceIdType.MESH
AXES = ("dp", "seq", "expert")


def _peer_coords(group, rank):
    coords = {a: lax.axis_index(a) for a in AXES}
    sizes = [lax.axis_size(a) for a in group]
    rest = rank
    for a, s in reversed(list(zip(group, sizes))):
        coords[a] = lax.rem(rest, s)
        rest = rest // s
    return tuple(coords[a] for a in AXES)


def _my_rank(group):
    rank = 0
    for a in group:
        rank = rank * lax.axis_size(a) + lax.axis_index(a)
    return rank


def _exchange_kernel(group, n, select, x_ref, o_ref, land, send_sem, recv_sem):
    me = _my_rank(group)
    barrier = pltpu.get_barrier_semaphore()
    for k in range(1, n):
        peer = _peer_coords(group, lax.rem(me + k, n))
        pl.semaphore_signal(barrier, inc=1, device_id=peer, device_id_type=MESH)
    pl.semaphore_wait(barrier, n - 1)

    def src_for(coords):
        if select is None:
            return x_ref
        return x_ref.at[coords[AXES.index(select)]]

    copies = []
    for k in range(1, n):
        peer = _peer_coords(group, lax.rem(me + k, n))
        copy = pltpu.make_async_remote_copy(
            src_ref=src_for(peer),
            dst_ref=land.at[me],
            send_sem=send_sem.at[k],
            recv_sem=recv_sem.at[k],
            device_id=peer,
            device_id_type=MESH,
        )
        copy.start()
        copies.append(copy)
    for copy in copies:
        copy.wait_send()
    for k in range(1, n):
        src_rank = lax.rem(me + n - k, n)
        pltpu.make_async_remote_copy(
            src_ref=src_for(_peer_coords(group, src_rank)),
            dst_ref=land.at[src_rank],
            send_sem=send_sem.at[k],
            recv_sem=recv_sem.at[k],
            device_id=_peer_coords(group, src_rank),
            device_id_type=MESH,
        ).wait_recv()
    o_ref[...] = land[...]
    own = src_for(_peer_coords(group, me))
    o_ref[me] = own[...]


def exchange(x, group, cid, select=None):
    n = 1
    for a in group:
        n *= lax.axis_size(a)
    block = x.shape if select is None else x.shape[1:]
    return pl.pallas_call(
        functools.partial(_exchange_kernel, group, n, select),
        out_shape=jax.ShapeDtypeStruct((n,) + block, x.dtype),
        in_specs=[pl.BlockSpec(memory_space=pltpu.VMEM)],
        out_specs=pl.BlockSpec(memory_space=pltpu.VMEM),
        scratch_shapes=[
            pltpu.VMEM((n,) + block, x.dtype),
            pltpu.SemaphoreType.DMA((n,)),
            pltpu.SemaphoreType.DMA((n,)),
        ],
        compiler_params=pltpu.CompilerParams(collective_id=cid, has_side_effects=True),
    )(x)


def _send_all(group, me, n, src_for, land, ssem, rsem):
    copies = []
    for k in range(1, n):
        peer = _peer_coords(group, lax.rem(me + k, n))
        copy = pltpu.make_async_remote_copy(
            src_ref=src_for(peer), dst_ref=land.at[me], send_sem=ssem.at[k],
            recv_sem=rsem.at[k], device_id=peer, device_id_type=MESH,
        )
        copy.start()
        copies.append(copy)
    return copies


def _wait_all(group, me, n, src_for, land, ssem, rsem, copies):
    for copy in copies:
        copy.wait_send()
    for k in range(1, n):
        src_rank = lax.rem(me + n - k, n)
        peer = _peer_coords(group, src_rank)
        pltpu.make_async_remote_copy(
            src_ref=src_for(peer), dst_ref=land.at[src_rank], send_sem=ssem.at[k],
            recv_sem=rsem.at[k], device_id=peer, device_id_type=MESH,
        ).wait_recv()


def _gelu(v):
    return 0.5 * v * (1.0 + jnp.tanh(0.7978845608028654 * (v + 0.044715 * v * v * v)))


def _slots_kernel(n_dp, n_seq, n_ex, tok_hbm, phi_ref, w_in_hbm, w_out_hbm,
                  phi_out, so_out, tok_v, num_ref, side_ref, w_in_v, w_out_v, w_sem,
                  num_land, side_land, phi_land, si_src, si_land, slot_in, part_src, pp_land,
                  cs_src, cs_land, so_src, so_land, sems):
    gs, gp, ge = ("seq",), ("dp",), ("expert",)
    me_s, me_p, me_e = _my_rank(gs), _my_rank(gp), _my_rank(ge)
    tok_copy = pltpu.make_async_copy(tok_hbm, tok_v, w_sem.at[2])
    tok_copy.start()
    w_in_copy = pltpu.make_async_copy(w_in_hbm, w_in_v, w_sem.at[0])
    w_out_copy = pltpu.make_async_copy(w_out_hbm, w_out_v, w_sem.at[1])
    w_in_copy.start()
    w_out_copy.start()

    barrier = pltpu.get_barrier_semaphore()
    for group, me, n in ((gs, me_s, n_seq), (gp, me_p, n_dp), (ge, me_e, n_ex)):
        for k in range(1, n):
            peer = _peer_coords(group, lax.rem(me + k, n))
            pl.semaphore_signal(barrier, inc=1, device_id=peer, device_id_type=MESH)

    tok_copy.wait()
    logits = lax.dot_general(
        phi_ref[...], tok_v[...], (((1,), (1,)), ((), ())), preferred_element_type=jnp.float32
    )
    local_max = jnp.max(logits, axis=1, keepdims=True)
    spread = jnp.exp(logits - local_max)
    denominator = jnp.sum(spread, axis=1, keepdims=True)
    num_ref[...] = jnp.dot(spread.astype(jnp.bfloat16), tok_v[...], preferred_element_type=jnp.float32)
    side_ref[:, 0:128] = jnp.broadcast_to(denominator, (denominator.shape[0], 128))
    side_ref[:, 128:256] = jnp.broadcast_to(local_max, (local_max.shape[0], 128))
    pl.semaphore_wait(barrier, n_seq - 1 + n_dp - 1 + n_ex - 1)

    stage_a = [
        (gs, me_s, n_seq, lambda c: num_ref, num_land, sems.at[0], sems.at[1]),
        (gs, me_s, n_seq, lambda c: side_ref, side_land, sems.at[2], sems.at[3]),
        (ge, me_e, n_ex, lambda c: phi_ref, phi_land, sems.at[4], sems.at[5]),
    ]
    started = [_send_all(*args) for args in stage_a]
    for args, copies in zip(stage_a[:2], started[:2]):
        _wait_all(*args, copies)
    num_land[me_s] = num_ref[...]
    side_land[me_s] = side_ref[...]

    side = side_land[...]
    part_max = side[:, :, 128:256]
    scale = jnp.exp(part_max - jnp.max(part_max, axis=0, keepdims=True))
    denom = jnp.sum(side[:, :, 0:128] * scale, axis=0)
    numer = jnp.sum(num_land[...] * scale[:, :, 0:1], axis=0)
    si_src[...] = (numer / denom[:, 0:1]).astype(si_src.dtype)

    stage_a2 = (gp, me_p, n_dp, lambda c: si_src, si_land, sems.at[6], sems.at[7])
    _wait_all(*stage_a2, _send_all(*stage_a2))
    si_land[me_p] = si_src[...]
    own_e = num_ref.shape[0]
    for c in range(n_dp):
        value = si_land[c].astype(jnp.float32)
        for e in range(own_e):
            slot_in[e, pl.ds(c, 1), :] = value[e:e + 1, :]

    w_in_copy.wait()
    w_out_copy.wait()
    for e in range(own_e):
        hidden = jnp.dot(slot_in[e].astype(jnp.bfloat16), w_in_v[e], preferred_element_type=jnp.float32)
        hidden = _gelu(hidden).astype(jnp.bfloat16)
        part = jnp.dot(hidden, w_out_v[e], preferred_element_type=jnp.float32)
        for c in range(n_dp):
            part_src[c, pl.ds(e, 1), :] = part[c:c + 1, :]

    dp_pos = AXES.index("dp")
    stage_b1 = (gp, me_p, n_dp, lambda c: part_src.at[c[dp_pos]], pp_land, sems.at[8], sems.at[9])
    _wait_all(*stage_b1, _send_all(*stage_b1))
    partner = lax.rem(me_p + 1, n_dp)
    cs_src[...] = part_src[me_p] + pp_land[partner]

    stage_b2 = (gs, me_s, n_seq, lambda c: cs_src, cs_land, sems.at[10], sems.at[11])
    _wait_all(*stage_b2, _send_all(*stage_b2))
    cs_land[me_s] = cs_src[...]
    so_src[...] = jnp.sum(cs_land[...], axis=0).astype(so_src.dtype)

    stage_c = (ge, me_e, n_ex, lambda c: so_src, so_land, sems.at[12], sems.at[13])
    _wait_all(*stage_c, _send_all(*stage_c))
    so_land[me_e] = so_src[...]
    so_out[...] = so_land[...]
    _wait_all(*stage_a[2], started[2])
    phi_land[me_e] = phi_ref[...]
    phi_out[...] = phi_land[...]


def expert_slots(tokens, phi_t, w_in, w_out, cid):
    n_dp, n_seq, n_ex = (lax.axis_size(a) for a in AXES)
    own_e, d = phi_t.shape
    vmem = pl.BlockSpec(memory_space=pltpu.VMEM)
    anywhere = pl.BlockSpec(memory_space=pl.ANY)
    gathered = jax.ShapeDtypeStruct((n_ex, own_e, d), jnp.bfloat16)
    return pl.pallas_call(
        functools.partial(_slots_kernel, n_dp, n_seq, n_ex),
        out_shape=(gathered, gathered),
        in_specs=[anywhere, vmem, anywhere, anywhere],
        out_specs=(vmem, vmem),
        scratch_shapes=[
            pltpu.VMEM(tokens.shape, tokens.dtype),
            pltpu.VMEM((own_e, d), jnp.float32),
            pltpu.VMEM((own_e, 256), jnp.float32),
            pltpu.VMEM(w_in.shape, w_in.dtype),
            pltpu.VMEM(w_out.shape, w_out.dtype),
            pltpu.SemaphoreType.DMA((3,)),
            pltpu.VMEM((n_seq, own_e, d), jnp.float32),
            pltpu.VMEM((n_seq, own_e, 256), jnp.float32),
            pltpu.VMEM((n_ex, own_e, d), jnp.bfloat16),
            pltpu.VMEM((own_e, d), jnp.bfloat16),
            pltpu.VMEM((n_dp, own_e, d), jnp.bfloat16),
            pltpu.VMEM((own_e, n_dp, d), jnp.float32),
            pltpu.VMEM((n_dp, own_e, d), jnp.float32),
            pltpu.VMEM((n_dp, own_e, d), jnp.float32),
            pltpu.VMEM((own_e, d), jnp.float32),
            pltpu.VMEM((n_seq, own_e, d), jnp.float32),
            pltpu.VMEM((own_e, d), jnp.bfloat16),
            pltpu.VMEM((n_ex, own_e, d), jnp.bfloat16),
            pltpu.SemaphoreType.DMA((14, max(n_dp, n_seq, n_ex))),
        ],
        compiler_params=pltpu.CompilerParams(
            collective_id=cid, has_side_effects=True, vmem_limit_bytes=48 * 1024 * 1024
        ),
    )(tokens, phi_t, w_in, w_out)

def on_device(tokens, phi, w_in, w_out):
    n_expert = lax.axis_size("expert")
    n_dp = lax.axis_size("dp")
    n_seq = lax.axis_size("seq")
    own_e = phi.shape[1]
    d = tokens.shape[1]
    rows_out = tokens.shape[0] // n_expert
    phi_g, slot_g = expert_slots(tokens, phi.T, w_in, w_out, 1)
    phi_all = phi_g.reshape(n_expert * own_e, d)
    slot_out = slot_g.reshape(n_expert * own_e, d)
    rows = lax.dynamic_slice_in_dim(tokens, lax.axis_index("expert") * rows_out, rows_out, 0)
    row_logits = lax.dot_general(
        phi_all, rows, (((1,), (1,)), ((), ())), preferred_element_type=jnp.float32
    )
    row_max = jnp.max(row_logits, axis=0)
    combine_weights = jnp.exp(row_logits - row_max[None, :])
    mixed_numer = lax.dot_general(
        combine_weights.astype(jnp.bfloat16),
        slot_out,
        (((0,), (0,)), ((), ())),
        preferred_element_type=jnp.float32,
    )
    mixed_denom = jnp.sum(combine_weights, axis=0)
    return (mixed_numer / mixed_denom[:, None]).astype(jnp.bfloat16)


def solution(mesh):
    placed = (
        P(("dp", "seq"), None),
        P(None, "expert"),
        P("expert", None, ("dp", "seq")),
        P("expert", ("dp", "seq"), None),
    )
    return jax.shard_map(
        on_device,
        mesh=mesh,
        in_specs=placed,
        out_specs=P(("dp", "seq", "expert"), None),
        check_vma=False,
    )
```

```python
import functools

import jax
import jax.numpy as jnp
from jax import lax
from jax.experimental import pallas as pl
from jax.experimental.pallas import tpu as pltpu
from jax.sharding import PartitionSpec as P

MESH = pl.DeviceIdType.MESH
AXES = ("dp", "seq", "expert")


def _peer_coords(group, rank):
    coords = {a: lax.axis_index(a) for a in AXES}
    sizes = [lax.axis_size(a) for a in group]
    rest = rank
    for a, s in reversed(list(zip(group, sizes))):
        coords[a] = lax.rem(rest, s)
        rest = rest // s
    return tuple(coords[a] for a in AXES)


def _my_rank(group):
    rank = 0
    for a in group:
        rank = rank * lax.axis_size(a) + lax.axis_index(a)
    return rank


def _exchange_kernel(group, n, select, x_ref, o_ref, land, send_sem, recv_sem):
    me = _my_rank(group)
    barrier = pltpu.get_barrier_semaphore()
    for k in range(1, n):
        peer = _peer_coords(group, lax.rem(me + k, n))
        pl.semaphore_signal(barrier, inc=1, device_id=peer, device_id_type=MESH)
    pl.semaphore_wait(barrier, n - 1)

    def src_for(coords):
        if select is None:
            return x_ref
        return x_ref.at[coords[AXES.index(select)]]

    copies = []
    for k in range(1, n):
        peer = _peer_coords(group, lax.rem(me + k, n))
        copy = pltpu.make_async_remote_copy(
            src_ref=src_for(peer),
            dst_ref=land.at[me],
            send_sem=send_sem.at[k],
            recv_sem=recv_sem.at[k],
            device_id=peer,
            device_id_type=MESH,
        )
        copy.start()
        copies.append(copy)
    for copy in copies:
        copy.wait_send()
    for k in range(1, n):
        src_rank = lax.rem(me + n - k, n)
        pltpu.make_async_remote_copy(
            src_ref=src_for(_peer_coords(group, src_rank)),
            dst_ref=land.at[src_rank],
            send_sem=send_sem.at[k],
            recv_sem=recv_sem.at[k],
            device_id=_peer_coords(group, src_rank),
            device_id_type=MESH,
        ).wait_recv()
    o_ref[...] = land[...]
    own = src_for(_peer_coords(group, me))
    o_ref[me] = own[...]


def exchange(x, group, cid, select=None):
    n = 1
    for a in group:
        n *= lax.axis_size(a)
    block = x.shape if select is None else x.shape[1:]
    return pl.pallas_call(
        functools.partial(_exchange_kernel, group, n, select),
        out_shape=jax.ShapeDtypeStruct((n,) + block, x.dtype),
        in_specs=[pl.BlockSpec(memory_space=pltpu.VMEM)],
        out_specs=pl.BlockSpec(memory_space=pltpu.VMEM),
        scratch_shapes=[
            pltpu.VMEM((n,) + block, x.dtype),
            pltpu.SemaphoreType.DMA((n,)),
            pltpu.SemaphoreType.DMA((n,)),
        ],
        compiler_params=pltpu.CompilerParams(collective_id=cid, has_side_effects=True),
    )(x)


def _send_all(group, me, n, src_for, land, ssem, rsem):
    copies = []
    for k in range(1, n):
        peer = _peer_coords(group, lax.rem(me + k, n))
        copy = pltpu.make_async_remote_copy(
            src_ref=src_for(peer), dst_ref=land.at[me], send_sem=ssem.at[k],
            recv_sem=rsem.at[k], device_id=peer, device_id_type=MESH,
        )
        copy.start()
        copies.append(copy)
    return copies


def _wait_all(group, me, n, src_for, land, ssem, rsem, copies):
    for copy in copies:
        copy.wait_send()
    for k in range(1, n):
        src_rank = lax.rem(me + n - k, n)
        peer = _peer_coords(group, src_rank)
        pltpu.make_async_remote_copy(
            src_ref=src_for(peer), dst_ref=land.at[src_rank], send_sem=ssem.at[k],
            recv_sem=rsem.at[k], device_id=peer, device_id_type=MESH,
        ).wait_recv()


def _gelu(v):
    return 0.5 * v * (1.0 + jnp.tanh(0.7978845608028654 * (v + 0.044715 * v * v * v)))


def _slots_kernel(n_dp, n_seq, n_ex, tok_hbm, phi_ref, w_in_hbm, w_out_hbm,
                  phi_out, so_out, tok_v, mx_ref, mx_land, num_ref, side_ref, w_in_v, w_out_v, w_sem,
                  num_land, side_land, phi_land, si_src, si_land, slot_in, part_src, pp_land,
                  cs_src, cs_land, so_src, so_land, sems):
    gs, gp, ge = ("seq",), ("dp",), ("expert",)
    me_s, me_p, me_e = _my_rank(gs), _my_rank(gp), _my_rank(ge)
    tok_copy = pltpu.make_async_copy(tok_hbm, tok_v, w_sem.at[2])
    tok_copy.start()
    w_in_copy = pltpu.make_async_copy(w_in_hbm, w_in_v, w_sem.at[0])
    w_out_copy = pltpu.make_async_copy(w_out_hbm, w_out_v, w_sem.at[1])
    w_in_copy.start()
    w_out_copy.start()

    barrier = pltpu.get_barrier_semaphore()
    for group, me, n in ((gs, me_s, n_seq), (gp, me_p, n_dp), (ge, me_e, n_ex)):
        for k in range(1, n):
            peer = _peer_coords(group, lax.rem(me + k, n))
            pl.semaphore_signal(barrier, inc=1, device_id=peer, device_id_type=MESH)

    tok_copy.wait()
    logits = lax.dot_general(
        phi_ref[...], tok_v[...], (((1,), (1,)), ((), ())), preferred_element_type=jnp.float32
    )
    mx_ref[...] = jnp.broadcast_to(jnp.max(logits, axis=1, keepdims=True), mx_ref.shape)
    pl.semaphore_wait(barrier, n_seq - 1 + n_dp - 1 + n_ex - 1)

    stage_a0 = (gs, me_s, n_seq, lambda c: mx_ref, mx_land, sems.at[14], sems.at[15])
    stage_phi = (ge, me_e, n_ex, lambda c: phi_ref, phi_land, sems.at[4], sems.at[5])
    started_a0 = _send_all(*stage_a0)
    started_phi = _send_all(*stage_phi)
    _wait_all(*stage_a0, started_a0)
    mx_land[me_s] = mx_ref[...]
    slot_max = jnp.max(mx_land[...], axis=0)[:, 0:1]
    spread = jnp.exp(logits - slot_max)
    denominator = jnp.sum(spread, axis=1, keepdims=True)
    num_ref[...] = jnp.dot(spread.astype(jnp.bfloat16), tok_v[...], preferred_element_type=jnp.float32)
    side_ref[...] = jnp.broadcast_to(denominator, side_ref.shape)

    stage_a = [
        (gs, me_s, n_seq, lambda c: num_ref, num_land, sems.at[0], sems.at[1]),
        (gs, me_s, n_seq, lambda c: side_ref, side_land, sems.at[2], sems.at[3]),
    ]
    started = [_send_all(*args) for args in stage_a]
    for args, copies in zip(stage_a, started):
        _wait_all(*args, copies)
    num_land[me_s] = num_ref[...]
    side_land[me_s] = side_ref[...]

    denom = jnp.sum(side_land[...], axis=0)
    numer = jnp.sum(num_land[...], axis=0)
    si_src[...] = (numer / denom[:, 0:1]).astype(si_src.dtype)

    stage_a2 = (gp, me_p, n_dp, lambda c: si_src, si_land, sems.at[6], sems.at[7])
    _wait_all(*stage_a2, _send_all(*stage_a2))
    si_land[me_p] = si_src[...]
    own_e = num_ref.shape[0]
    for c in range(n_dp):
        value = si_land[c].astype(jnp.float32)
        for e in range(own_e):
            slot_in[e, pl.ds(c, 1), :] = value[e:e + 1, :]

    w_in_copy.wait()
    w_out_copy.wait()
    for e in range(own_e):
        hidden = jnp.dot(slot_in[e].astype(jnp.bfloat16), w_in_v[e], preferred_element_type=jnp.float32)
        hidden = _gelu(hidden).astype(jnp.bfloat16)
        part = jnp.dot(hidden, w_out_v[e], preferred_element_type=jnp.float32)
        for c in range(n_dp):
            part_src[c, pl.ds(e, 1), :] = part[c:c + 1, :]

    dp_pos = AXES.index("dp")
    stage_b1 = (gp, me_p, n_dp, lambda c: part_src.at[c[dp_pos]], pp_land, sems.at[8], sems.at[9])
    _wait_all(*stage_b1, _send_all(*stage_b1))
    partner = lax.rem(me_p + 1, n_dp)
    cs_src[...] = part_src[me_p] + pp_land[partner]

    stage_b2 = (gs, me_s, n_seq, lambda c: cs_src, cs_land, sems.at[10], sems.at[11])
    _wait_all(*stage_b2, _send_all(*stage_b2))
    cs_land[me_s] = cs_src[...]
    so_src[...] = jnp.sum(cs_land[...], axis=0).astype(so_src.dtype)

    stage_c = (ge, me_e, n_ex, lambda c: so_src, so_land, sems.at[12], sems.at[13])
    _wait_all(*stage_c, _send_all(*stage_c))
    so_land[me_e] = so_src[...]
    so_out[...] = so_land[...]
    _wait_all(*stage_phi, started_phi)
    phi_land[me_e] = phi_ref[...]
    phi_out[...] = phi_land[...]


def expert_slots(tokens, phi_t, w_in, w_out, cid):
    n_dp, n_seq, n_ex = (lax.axis_size(a) for a in AXES)
    own_e, d = phi_t.shape
    vmem = pl.BlockSpec(memory_space=pltpu.VMEM)
    anywhere = pl.BlockSpec(memory_space=pl.ANY)
    gathered = jax.ShapeDtypeStruct((n_ex, own_e, d), jnp.bfloat16)
    return pl.pallas_call(
        functools.partial(_slots_kernel, n_dp, n_seq, n_ex),
        out_shape=(gathered, gathered),
        in_specs=[anywhere, vmem, anywhere, anywhere],
        out_specs=(vmem, vmem),
        scratch_shapes=[
            pltpu.VMEM(tokens.shape, tokens.dtype),
            pltpu.VMEM((own_e, 128), jnp.float32),
            pltpu.VMEM((n_seq, own_e, 128), jnp.float32),
            pltpu.VMEM((own_e, d), jnp.float32),
            pltpu.VMEM((own_e, 128), jnp.float32),
            pltpu.VMEM(w_in.shape, w_in.dtype),
            pltpu.VMEM(w_out.shape, w_out.dtype),
            pltpu.SemaphoreType.DMA((3,)),
            pltpu.VMEM((n_seq, own_e, d), jnp.float32),
            pltpu.VMEM((n_seq, own_e, 128), jnp.float32),
            pltpu.VMEM((n_ex, own_e, d), jnp.bfloat16),
            pltpu.VMEM((own_e, d), jnp.bfloat16),
            pltpu.VMEM((n_dp, own_e, d), jnp.bfloat16),
            pltpu.VMEM((own_e, n_dp, d), jnp.float32),
            pltpu.VMEM((n_dp, own_e, d), jnp.float32),
            pltpu.VMEM((n_dp, own_e, d), jnp.float32),
            pltpu.VMEM((own_e, d), jnp.float32),
            pltpu.VMEM((n_seq, own_e, d), jnp.float32),
            pltpu.VMEM((own_e, d), jnp.bfloat16),
            pltpu.VMEM((n_ex, own_e, d), jnp.bfloat16),
            pltpu.SemaphoreType.DMA((16, max(n_dp, n_seq, n_ex))),
        ],
        compiler_params=pltpu.CompilerParams(
            collective_id=cid, has_side_effects=True, vmem_limit_bytes=48 * 1024 * 1024
        ),
    )(tokens, phi_t, w_in, w_out)

def on_device(tokens, phi, w_in, w_out):
    n_expert = lax.axis_size("expert")
    n_dp = lax.axis_size("dp")
    n_seq = lax.axis_size("seq")
    own_e = phi.shape[1]
    d = tokens.shape[1]
    rows_out = tokens.shape[0] // n_expert
    phi_g, slot_g = expert_slots(tokens, phi.T, w_in, w_out, 1)
    phi_all = phi_g.reshape(n_expert * own_e, d)
    slot_out = slot_g.reshape(n_expert * own_e, d)
    rows = lax.dynamic_slice_in_dim(tokens, lax.axis_index("expert") * rows_out, rows_out, 0)
    row_logits = lax.dot_general(
        phi_all, rows, (((1,), (1,)), ((), ())), preferred_element_type=jnp.float32
    )
    row_max = jnp.max(row_logits, axis=0)
    combine_weights = jnp.exp(row_logits - row_max[None, :])
    mixed_numer = lax.dot_general(
        combine_weights.astype(jnp.bfloat16),
        slot_out,
        (((0,), (0,)), ((), ())),
        preferred_element_type=jnp.float32,
    )
    mixed_denom = jnp.sum(combine_weights, axis=0)
    return (mixed_numer / mixed_denom[:, None]).astype(jnp.bfloat16)


def solution(mesh):
    placed = (
        P(("dp", "seq"), None),
        P(None, "expert"),
        P("expert", None, ("dp", "seq")),
        P("expert", ("dp", "seq"), None),
    )
    return jax.shard_map(
        on_device,
        mesh=mesh,
        in_specs=placed,
        out_specs=P(("dp", "seq", "expert"), None),
        check_vma=False,
    )
```

```python
import functools

import jax
import jax.numpy as jnp
from jax import lax
from jax.experimental import pallas as pl
from jax.experimental.pallas import tpu as pltpu
from jax.sharding import PartitionSpec as P

MESH = pl.DeviceIdType.MESH
AXES = ("dp", "seq", "expert")


def _peer_coords(group, rank):
    coords = {a: lax.axis_index(a) for a in AXES}
    sizes = [lax.axis_size(a) for a in group]
    rest = rank
    for a, s in reversed(list(zip(group, sizes))):
        coords[a] = lax.rem(rest, s)
        rest = rest // s
    return tuple(coords[a] for a in AXES)


def _my_rank(group):
    rank = 0
    for a in group:
        rank = rank * lax.axis_size(a) + lax.axis_index(a)
    return rank


def _exchange_kernel(group, n, select, x_ref, o_ref, land, send_sem, recv_sem):
    me = _my_rank(group)
    barrier = pltpu.get_barrier_semaphore()
    for k in range(1, n):
        peer = _peer_coords(group, lax.rem(me + k, n))
        pl.semaphore_signal(barrier, inc=1, device_id=peer, device_id_type=MESH)
    pl.semaphore_wait(barrier, n - 1)

    def src_for(coords):
        if select is None:
            return x_ref
        return x_ref.at[coords[AXES.index(select)]]

    copies = []
    for k in range(1, n):
        peer = _peer_coords(group, lax.rem(me + k, n))
        copy = pltpu.make_async_remote_copy(
            src_ref=src_for(peer),
            dst_ref=land.at[me],
            send_sem=send_sem.at[k],
            recv_sem=recv_sem.at[k],
            device_id=peer,
            device_id_type=MESH,
        )
        copy.start()
        copies.append(copy)
    for copy in copies:
        copy.wait_send()
    for k in range(1, n):
        src_rank = lax.rem(me + n - k, n)
        pltpu.make_async_remote_copy(
            src_ref=src_for(_peer_coords(group, src_rank)),
            dst_ref=land.at[src_rank],
            send_sem=send_sem.at[k],
            recv_sem=recv_sem.at[k],
            device_id=_peer_coords(group, src_rank),
            device_id_type=MESH,
        ).wait_recv()
    o_ref[...] = land[...]
    own = src_for(_peer_coords(group, me))
    o_ref[me] = own[...]


def exchange(x, group, cid, select=None):
    n = 1
    for a in group:
        n *= lax.axis_size(a)
    block = x.shape if select is None else x.shape[1:]
    return pl.pallas_call(
        functools.partial(_exchange_kernel, group, n, select),
        out_shape=jax.ShapeDtypeStruct((n,) + block, x.dtype),
        in_specs=[pl.BlockSpec(memory_space=pltpu.VMEM)],
        out_specs=pl.BlockSpec(memory_space=pltpu.VMEM),
        scratch_shapes=[
            pltpu.VMEM((n,) + block, x.dtype),
            pltpu.SemaphoreType.DMA((n,)),
            pltpu.SemaphoreType.DMA((n,)),
        ],
        compiler_params=pltpu.CompilerParams(collective_id=cid, has_side_effects=True),
    )(x)


def _send_all(group, me, n, src_for, land, ssem, rsem):
    copies = []
    for k in range(1, n):
        peer = _peer_coords(group, lax.rem(me + k, n))
        copy = pltpu.make_async_remote_copy(
            src_ref=src_for(peer), dst_ref=land.at[me], send_sem=ssem.at[k],
            recv_sem=rsem.at[k], device_id=peer, device_id_type=MESH,
        )
        copy.start()
        copies.append(copy)
    return copies


def _wait_all(group, me, n, src_for, land, ssem, rsem, copies):
    for copy in copies:
        copy.wait_send()
    for k in range(1, n):
        src_rank = lax.rem(me + n - k, n)
        peer = _peer_coords(group, src_rank)
        pltpu.make_async_remote_copy(
            src_ref=src_for(peer), dst_ref=land.at[src_rank], send_sem=ssem.at[k],
            recv_sem=rsem.at[k], device_id=peer, device_id_type=MESH,
        ).wait_recv()


def _gelu(v):
    return 0.5 * v * (1.0 + jnp.tanh(0.7978845608028654 * (v + 0.044715 * v * v * v)))


def _slots_kernel(n_dp, n_seq, n_ex, tok_hbm, phi_ref, w_in_hbm, w_out_hbm,
                  lg_out, so_out, tok_v, mx_ref, mx_land, num_ref, side_ref, w_in_v, w_out_v, w_sem,
                  num_land, side_land, lg_src, lg_land, si_src, si_land, slot_in, part_src, pp_land,
                  cs_src, cs_land, so_src, so_land, sems):
    gs, gp, ge = ("seq",), ("dp",), ("expert",)
    me_s, me_p, me_e = _my_rank(gs), _my_rank(gp), _my_rank(ge)
    tok_copy = pltpu.make_async_copy(tok_hbm, tok_v, w_sem.at[2])
    tok_copy.start()
    w_in_copy = pltpu.make_async_copy(w_in_hbm, w_in_v, w_sem.at[0])
    w_out_copy = pltpu.make_async_copy(w_out_hbm, w_out_v, w_sem.at[1])
    w_in_copy.start()
    w_out_copy.start()

    barrier = pltpu.get_barrier_semaphore()
    for group, me, n in ((gs, me_s, n_seq), (gp, me_p, n_dp), (ge, me_e, n_ex)):
        for k in range(1, n):
            peer = _peer_coords(group, lax.rem(me + k, n))
            pl.semaphore_signal(barrier, inc=1, device_id=peer, device_id_type=MESH)

    tok_copy.wait()
    logits = lax.dot_general(
        phi_ref[...], tok_v[...], (((1,), (1,)), ((), ())), preferred_element_type=jnp.float32
    )
    mx_ref[...] = jnp.broadcast_to(jnp.max(logits, axis=1, keepdims=True), mx_ref.shape)
    rows_out = lg_src.shape[2]
    for g in range(n_ex):
        lg_src[g] = logits[:, g * rows_out:(g + 1) * rows_out]
    pl.semaphore_wait(barrier, n_seq - 1 + n_dp - 1 + n_ex - 1)

    stage_a0 = (gs, me_s, n_seq, lambda c: mx_ref, mx_land, sems.at[14], sems.at[15])
    ex_pos = AXES.index("expert")
    stage_phi = (ge, me_e, n_ex, lambda c: lg_src.at[c[ex_pos]], lg_land, sems.at[4], sems.at[5])
    started_a0 = _send_all(*stage_a0)
    started_phi = _send_all(*stage_phi)
    _wait_all(*stage_a0, started_a0)
    mx_land[me_s] = mx_ref[...]
    slot_max = jnp.max(mx_land[...], axis=0)[:, 0:1]
    spread = jnp.exp(logits - slot_max)
    denominator = jnp.sum(spread, axis=1, keepdims=True)
    num_ref[...] = jnp.dot(spread.astype(jnp.bfloat16), tok_v[...], preferred_element_type=jnp.float32)
    side_ref[...] = jnp.broadcast_to(denominator, side_ref.shape)

    stage_a = [
        (gs, me_s, n_seq, lambda c: num_ref, num_land, sems.at[0], sems.at[1]),
        (gs, me_s, n_seq, lambda c: side_ref, side_land, sems.at[2], sems.at[3]),
    ]
    started = [_send_all(*args) for args in stage_a]
    for args, copies in zip(stage_a, started):
        _wait_all(*args, copies)
    num_land[me_s] = num_ref[...]
    side_land[me_s] = side_ref[...]

    denom = jnp.sum(side_land[...], axis=0)
    numer = jnp.sum(num_land[...], axis=0)
    si_src[...] = (numer / denom[:, 0:1]).astype(si_src.dtype)

    stage_a2 = (gp, me_p, n_dp, lambda c: si_src, si_land, sems.at[6], sems.at[7])
    _wait_all(*stage_a2, _send_all(*stage_a2))
    si_land[me_p] = si_src[...]
    own_e = num_ref.shape[0]
    for c in range(n_dp):
        value = si_land[c].astype(jnp.float32)
        for e in range(own_e):
            slot_in[e, pl.ds(c, 1), :] = value[e:e + 1, :]

    w_in_copy.wait()
    w_out_copy.wait()
    for e in range(own_e):
        hidden = jnp.dot(slot_in[e].astype(jnp.bfloat16), w_in_v[e], preferred_element_type=jnp.float32)
        hidden = _gelu(hidden).astype(jnp.bfloat16)
        part = jnp.dot(hidden, w_out_v[e], preferred_element_type=jnp.float32)
        for c in range(n_dp):
            part_src[c, pl.ds(e, 1), :] = part[c:c + 1, :]

    dp_pos = AXES.index("dp")
    stage_b1 = (gp, me_p, n_dp, lambda c: part_src.at[c[dp_pos]], pp_land, sems.at[8], sems.at[9])
    _wait_all(*stage_b1, _send_all(*stage_b1))
    partner = lax.rem(me_p + 1, n_dp)
    cs_src[...] = part_src[me_p] + pp_land[partner]

    stage_b2 = (gs, me_s, n_seq, lambda c: cs_src, cs_land, sems.at[10], sems.at[11])
    _wait_all(*stage_b2, _send_all(*stage_b2))
    cs_land[me_s] = cs_src[...]
    so_src[...] = jnp.sum(cs_land[...], axis=0).astype(so_src.dtype)

    stage_c = (ge, me_e, n_ex, lambda c: so_src, so_land, sems.at[12], sems.at[13])
    _wait_all(*stage_c, _send_all(*stage_c))
    so_land[me_e] = so_src[...]
    so_out[...] = so_land[...]
    _wait_all(*stage_phi, started_phi)
    lg_land[me_e] = lg_src[me_e]
    lg_out[...] = lg_land[...]


def expert_slots(tokens, phi_t, w_in, w_out, cid):
    n_dp, n_seq, n_ex = (lax.axis_size(a) for a in AXES)
    own_e, d = phi_t.shape
    vmem = pl.BlockSpec(memory_space=pltpu.VMEM)
    anywhere = pl.BlockSpec(memory_space=pl.ANY)
    gathered = jax.ShapeDtypeStruct((n_ex, own_e, d), jnp.bfloat16)
    rows_out = tokens.shape[0] // n_ex
    row_logits = jax.ShapeDtypeStruct((n_ex, own_e, rows_out), jnp.float32)
    return pl.pallas_call(
        functools.partial(_slots_kernel, n_dp, n_seq, n_ex),
        out_shape=(row_logits, gathered),
        in_specs=[anywhere, vmem, anywhere, anywhere],
        out_specs=(vmem, vmem),
        scratch_shapes=[
            pltpu.VMEM(tokens.shape, tokens.dtype),
            pltpu.VMEM((own_e, 128), jnp.float32),
            pltpu.VMEM((n_seq, own_e, 128), jnp.float32),
            pltpu.VMEM((own_e, d), jnp.float32),
            pltpu.VMEM((own_e, 128), jnp.float32),
            pltpu.VMEM(w_in.shape, w_in.dtype),
            pltpu.VMEM(w_out.shape, w_out.dtype),
            pltpu.SemaphoreType.DMA((3,)),
            pltpu.VMEM((n_seq, own_e, d), jnp.float32),
            pltpu.VMEM((n_seq, own_e, 128), jnp.float32),
            pltpu.VMEM((n_ex, own_e, rows_out), jnp.float32),
            pltpu.VMEM((n_ex, own_e, rows_out), jnp.float32),
            pltpu.VMEM((own_e, d), jnp.bfloat16),
            pltpu.VMEM((n_dp, own_e, d), jnp.bfloat16),
            pltpu.VMEM((own_e, n_dp, d), jnp.float32),
            pltpu.VMEM((n_dp, own_e, d), jnp.float32),
            pltpu.VMEM((n_dp, own_e, d), jnp.float32),
            pltpu.VMEM((own_e, d), jnp.float32),
            pltpu.VMEM((n_seq, own_e, d), jnp.float32),
            pltpu.VMEM((own_e, d), jnp.bfloat16),
            pltpu.VMEM((n_ex, own_e, d), jnp.bfloat16),
            pltpu.SemaphoreType.DMA((16, max(n_dp, n_seq, n_ex))),
        ],
        compiler_params=pltpu.CompilerParams(
            collective_id=cid, has_side_effects=True, vmem_limit_bytes=48 * 1024 * 1024
        ),
    )(tokens, phi_t, w_in, w_out)

def on_device(tokens, phi, w_in, w_out):
    n_expert = lax.axis_size("expert")
    n_dp = lax.axis_size("dp")
    n_seq = lax.axis_size("seq")
    own_e = phi.shape[1]
    d = tokens.shape[1]
    rows_out = tokens.shape[0] // n_expert
    logit_g, slot_g = expert_slots(tokens, phi.T, w_in, w_out, 1)
    row_logits = logit_g.reshape(n_expert * own_e, rows_out)
    slot_out = slot_g.reshape(n_expert * own_e, d)
    row_max = jnp.max(row_logits, axis=0)
    combine_weights = jnp.exp(row_logits - row_max[None, :])
    mixed_numer = lax.dot_general(
        combine_weights.astype(jnp.bfloat16),
        slot_out,
        (((0,), (0,)), ((), ())),
        preferred_element_type=jnp.float32,
    )
    mixed_denom = jnp.sum(combine_weights, axis=0)
    return (mixed_numer / mixed_denom[:, None]).astype(jnp.bfloat16)


def solution(mesh):
    placed = (
        P(("dp", "seq"), None),
        P(None, "expert"),
        P("expert", None, ("dp", "seq")),
        P("expert", ("dp", "seq"), None),
    )
    return jax.shard_map(
        on_device,
        mesh=mesh,
        in_specs=placed,
        out_specs=P(("dp", "seq", "expert"), None),
        check_vma=False,
    )
```

```python
import functools

import jax
import jax.numpy as jnp
from jax import lax
from jax.experimental import pallas as pl
from jax.experimental.pallas import tpu as pltpu
from jax.sharding import PartitionSpec as P

MESH = pl.DeviceIdType.MESH
AXES = ("dp", "seq", "expert")


def _peer_coords(group, rank):
    coords = {a: lax.axis_index(a) for a in AXES}
    sizes = [lax.axis_size(a) for a in group]
    rest = rank
    for a, s in reversed(list(zip(group, sizes))):
        coords[a] = lax.rem(rest, s)
        rest = rest // s
    return tuple(coords[a] for a in AXES)


def _my_rank(group):
    rank = 0
    for a in group:
        rank = rank * lax.axis_size(a) + lax.axis_index(a)
    return rank


def _exchange_kernel(group, n, select, x_ref, o_ref, land, send_sem, recv_sem):
    me = _my_rank(group)
    barrier = pltpu.get_barrier_semaphore()
    for k in range(1, n):
        peer = _peer_coords(group, lax.rem(me + k, n))
        pl.semaphore_signal(barrier, inc=1, device_id=peer, device_id_type=MESH)
    pl.semaphore_wait(barrier, n - 1)

    def src_for(coords):
        if select is None:
            return x_ref
        return x_ref.at[coords[AXES.index(select)]]

    copies = []
    for k in range(1, n):
        peer = _peer_coords(group, lax.rem(me + k, n))
        copy = pltpu.make_async_remote_copy(
            src_ref=src_for(peer),
            dst_ref=land.at[me],
            send_sem=send_sem.at[k],
            recv_sem=recv_sem.at[k],
            device_id=peer,
            device_id_type=MESH,
        )
        copy.start()
        copies.append(copy)
    for copy in copies:
        copy.wait_send()
    for k in range(1, n):
        src_rank = lax.rem(me + n - k, n)
        pltpu.make_async_remote_copy(
            src_ref=src_for(_peer_coords(group, src_rank)),
            dst_ref=land.at[src_rank],
            send_sem=send_sem.at[k],
            recv_sem=recv_sem.at[k],
            device_id=_peer_coords(group, src_rank),
            device_id_type=MESH,
        ).wait_recv()
    o_ref[...] = land[...]
    own = src_for(_peer_coords(group, me))
    o_ref[me] = own[...]


def exchange(x, group, cid, select=None):
    n = 1
    for a in group:
        n *= lax.axis_size(a)
    block = x.shape if select is None else x.shape[1:]
    return pl.pallas_call(
        functools.partial(_exchange_kernel, group, n, select),
        out_shape=jax.ShapeDtypeStruct((n,) + block, x.dtype),
        in_specs=[pl.BlockSpec(memory_space=pltpu.VMEM)],
        out_specs=pl.BlockSpec(memory_space=pltpu.VMEM),
        scratch_shapes=[
            pltpu.VMEM((n,) + block, x.dtype),
            pltpu.SemaphoreType.DMA((n,)),
            pltpu.SemaphoreType.DMA((n,)),
        ],
        compiler_params=pltpu.CompilerParams(collective_id=cid, has_side_effects=True),
    )(x)


def _send_all(group, me, n, src_for, land, ssem, rsem):
    copies = []
    for k in range(1, n):
        peer = _peer_coords(group, lax.rem(me + k, n))
        copy = pltpu.make_async_remote_copy(
            src_ref=src_for(peer), dst_ref=land.at[me], send_sem=ssem.at[k],
            recv_sem=rsem.at[k], device_id=peer, device_id_type=MESH,
        )
        copy.start()
        copies.append(copy)
    return copies


def _wait_all(group, me, n, src_for, land, ssem, rsem, copies):
    for copy in copies:
        copy.wait_send()
    for k in range(1, n):
        src_rank = lax.rem(me + n - k, n)
        peer = _peer_coords(group, src_rank)
        pltpu.make_async_remote_copy(
            src_ref=src_for(peer), dst_ref=land.at[src_rank], send_sem=ssem.at[k],
            recv_sem=rsem.at[k], device_id=peer, device_id_type=MESH,
        ).wait_recv()


def _gelu(v):
    return 0.5 * v * (1.0 + jnp.tanh(0.7978845608028654 * (v + 0.044715 * v * v * v)))


def _slots_kernel(n_dp, n_seq, n_ex, tok_v, phi_ref, w_in_hbm, w_out_hbm,
                  lg_out, so_out, mx_ref, mx_land, num_ref, side_ref, w_in_v, w_out_v, w_sem,
                  num_land, side_land, lg_src, lg_land, si_src, si_land, slot_in, part_src, pp_land,
                  cs_src, cs_land, so_src, so_land, sems):
    gs, gp, ge = ("seq",), ("dp",), ("expert",)
    me_s, me_p, me_e = _my_rank(gs), _my_rank(gp), _my_rank(ge)
    w_in_copy = pltpu.make_async_copy(w_in_hbm, w_in_v, w_sem.at[0])
    w_out_copy = pltpu.make_async_copy(w_out_hbm, w_out_v, w_sem.at[1])
    w_in_copy.start()
    w_out_copy.start()

    barrier = pltpu.get_barrier_semaphore()
    for group, me, n in ((gs, me_s, n_seq), (gp, me_p, n_dp), (ge, me_e, n_ex)):
        for k in range(1, n):
            peer = _peer_coords(group, lax.rem(me + k, n))
            pl.semaphore_signal(barrier, inc=1, device_id=peer, device_id_type=MESH)

    logits = lax.dot_general(
        phi_ref[...], tok_v[...], (((1,), (1,)), ((), ())), preferred_element_type=jnp.float32
    )
    mx_ref[...] = jnp.broadcast_to(jnp.max(logits, axis=1, keepdims=True), mx_ref.shape)
    rows_out = lg_src.shape[2]
    for g in range(n_ex):
        lg_src[g] = logits[:, g * rows_out:(g + 1) * rows_out]
    pl.semaphore_wait(barrier, n_seq - 1 + n_dp - 1 + n_ex - 1)

    stage_a0 = (gs, me_s, n_seq, lambda c: mx_ref, mx_land, sems.at[14], sems.at[15])
    ex_pos = AXES.index("expert")
    stage_phi = (ge, me_e, n_ex, lambda c: lg_src.at[c[ex_pos]], lg_land, sems.at[4], sems.at[5])
    started_a0 = _send_all(*stage_a0)
    started_phi = _send_all(*stage_phi)
    _wait_all(*stage_a0, started_a0)
    mx_land[me_s] = mx_ref[...]
    slot_max = jnp.max(mx_land[...], axis=0)[:, 0:1]
    spread = jnp.exp(logits - slot_max)
    denominator = jnp.sum(spread, axis=1, keepdims=True)
    num_ref[...] = jnp.dot(spread.astype(jnp.bfloat16), tok_v[...], preferred_element_type=jnp.float32)
    side_ref[...] = jnp.broadcast_to(denominator, side_ref.shape)

    stage_a = [
        (gs, me_s, n_seq, lambda c: num_ref, num_land, sems.at[0], sems.at[1]),
        (gs, me_s, n_seq, lambda c: side_ref, side_land, sems.at[2], sems.at[3]),
    ]
    started = [_send_all(*args) for args in stage_a]
    for args, copies in zip(stage_a, started):
        _wait_all(*args, copies)
    num_land[me_s] = num_ref[...]
    side_land[me_s] = side_ref[...]

    denom = jnp.sum(side_land[...], axis=0)
    numer = jnp.sum(num_land[...], axis=0)
    si_src[...] = (numer / denom[:, 0:1]).astype(si_src.dtype)

    stage_a2 = (gp, me_p, n_dp, lambda c: si_src, si_land, sems.at[6], sems.at[7])
    _wait_all(*stage_a2, _send_all(*stage_a2))
    si_land[me_p] = si_src[...]
    own_e = num_ref.shape[0]
    for c in range(n_dp):
        value = si_land[c].astype(jnp.float32)
        for e in range(own_e):
            slot_in[e, pl.ds(c, 1), :] = value[e:e + 1, :]

    w_in_copy.wait()
    w_out_copy.wait()
    for e in range(own_e):
        hidden = jnp.dot(slot_in[e].astype(jnp.bfloat16), w_in_v[e], preferred_element_type=jnp.float32)
        hidden = _gelu(hidden).astype(jnp.bfloat16)
        part = jnp.dot(hidden, w_out_v[e], preferred_element_type=jnp.float32)
        for c in range(n_dp):
            part_src[c, pl.ds(e, 1), :] = part[c:c + 1, :]

    dp_pos = AXES.index("dp")
    stage_b1 = (gp, me_p, n_dp, lambda c: part_src.at[c[dp_pos]], pp_land, sems.at[8], sems.at[9])
    _wait_all(*stage_b1, _send_all(*stage_b1))
    partner = lax.rem(me_p + 1, n_dp)
    cs_src[...] = part_src[me_p] + pp_land[partner]

    stage_b2 = (gs, me_s, n_seq, lambda c: cs_src, cs_land, sems.at[10], sems.at[11])
    _wait_all(*stage_b2, _send_all(*stage_b2))
    cs_land[me_s] = cs_src[...]
    so_src[...] = jnp.sum(cs_land[...], axis=0).astype(so_src.dtype)

    stage_c = (ge, me_e, n_ex, lambda c: so_src, so_land, sems.at[12], sems.at[13])
    _wait_all(*stage_c, _send_all(*stage_c))
    so_land[me_e] = so_src[...]
    so_out[...] = so_land[...]
    _wait_all(*stage_phi, started_phi)
    lg_land[me_e] = lg_src[me_e]
    lg_out[...] = lg_land[...]


def expert_slots(tokens, phi_t, w_in, w_out, cid):
    n_dp, n_seq, n_ex = (lax.axis_size(a) for a in AXES)
    own_e, d = phi_t.shape
    vmem = pl.BlockSpec(memory_space=pltpu.VMEM)
    anywhere = pl.BlockSpec(memory_space=pl.ANY)
    gathered = jax.ShapeDtypeStruct((n_ex, own_e, d), jnp.bfloat16)
    rows_out = tokens.shape[0] // n_ex
    row_logits = jax.ShapeDtypeStruct((n_ex, own_e, rows_out), jnp.float32)
    return pl.pallas_call(
        functools.partial(_slots_kernel, n_dp, n_seq, n_ex),
        out_shape=(row_logits, gathered),
        in_specs=[vmem, vmem, anywhere, anywhere],
        out_specs=(vmem, vmem),
        scratch_shapes=[
            pltpu.VMEM((own_e, 128), jnp.float32),
            pltpu.VMEM((n_seq, own_e, 128), jnp.float32),
            pltpu.VMEM((own_e, d), jnp.float32),
            pltpu.VMEM((own_e, 128), jnp.float32),
            pltpu.VMEM(w_in.shape, w_in.dtype),
            pltpu.VMEM(w_out.shape, w_out.dtype),
            pltpu.SemaphoreType.DMA((2,)),
            pltpu.VMEM((n_seq, own_e, d), jnp.float32),
            pltpu.VMEM((n_seq, own_e, 128), jnp.float32),
            pltpu.VMEM((n_ex, own_e, rows_out), jnp.float32),
            pltpu.VMEM((n_ex, own_e, rows_out), jnp.float32),
            pltpu.VMEM((own_e, d), jnp.bfloat16),
            pltpu.VMEM((n_dp, own_e, d), jnp.bfloat16),
            pltpu.VMEM((own_e, n_dp, d), jnp.float32),
            pltpu.VMEM((n_dp, own_e, d), jnp.float32),
            pltpu.VMEM((n_dp, own_e, d), jnp.float32),
            pltpu.VMEM((own_e, d), jnp.float32),
            pltpu.VMEM((n_seq, own_e, d), jnp.float32),
            pltpu.VMEM((own_e, d), jnp.bfloat16),
            pltpu.VMEM((n_ex, own_e, d), jnp.bfloat16),
            pltpu.SemaphoreType.DMA((16, max(n_dp, n_seq, n_ex))),
        ],
        compiler_params=pltpu.CompilerParams(
            collective_id=cid, has_side_effects=True, vmem_limit_bytes=48 * 1024 * 1024
        ),
    )(tokens, phi_t, w_in, w_out)

def on_device(tokens, phi, w_in, w_out):
    n_expert = lax.axis_size("expert")
    n_dp = lax.axis_size("dp")
    n_seq = lax.axis_size("seq")
    own_e = phi.shape[1]
    d = tokens.shape[1]
    rows_out = tokens.shape[0] // n_expert
    logit_g, slot_g = expert_slots(tokens, phi.T, w_in, w_out, 1)
    row_logits = logit_g.reshape(n_expert * own_e, rows_out)
    slot_out = slot_g.reshape(n_expert * own_e, d)
    row_max = jnp.max(row_logits, axis=0)
    combine_weights = jnp.exp(row_logits - row_max[None, :])
    mixed_numer = lax.dot_general(
        combine_weights.astype(jnp.bfloat16),
        slot_out,
        (((0,), (0,)), ((), ())),
        preferred_element_type=jnp.float32,
    )
    mixed_denom = jnp.sum(combine_weights, axis=0)
    return (mixed_numer / mixed_denom[:, None]).astype(jnp.bfloat16)


def solution(mesh):
    placed = (
        P(("dp", "seq"), None),
        P(None, "expert"),
        P("expert", None, ("dp", "seq")),
        P("expert", ("dp", "seq"), None),
    )
    return jax.shard_map(
        on_device,
        mesh=mesh,
        in_specs=placed,
        out_specs=P(("dp", "seq", "expert"), None),
        check_vma=False,
    )
```

```python
import functools

import jax
import jax.numpy as jnp
from jax import lax
from jax.experimental import pallas as pl
from jax.experimental.pallas import tpu as pltpu
from jax.sharding import PartitionSpec as P

MESH = pl.DeviceIdType.MESH
AXES = ("dp", "seq", "expert")


def _peer_coords(group, rank):
    coords = {a: lax.axis_index(a) for a in AXES}
    sizes = [lax.axis_size(a) for a in group]
    rest = rank
    for a, s in reversed(list(zip(group, sizes))):
        coords[a] = lax.rem(rest, s)
        rest = rest // s
    return tuple(coords[a] for a in AXES)


def _my_rank(group):
    rank = 0
    for a in group:
        rank = rank * lax.axis_size(a) + lax.axis_index(a)
    return rank


def _exchange_kernel(group, n, select, x_ref, o_ref, land, send_sem, recv_sem):
    me = _my_rank(group)
    barrier = pltpu.get_barrier_semaphore()
    for k in range(1, n):
        peer = _peer_coords(group, lax.rem(me + k, n))
        pl.semaphore_signal(barrier, inc=1, device_id=peer, device_id_type=MESH)
    pl.semaphore_wait(barrier, n - 1)

    def src_for(coords):
        if select is None:
            return x_ref
        return x_ref.at[coords[AXES.index(select)]]

    copies = []
    for k in range(1, n):
        peer = _peer_coords(group, lax.rem(me + k, n))
        copy = pltpu.make_async_remote_copy(
            src_ref=src_for(peer),
            dst_ref=land.at[me],
            send_sem=send_sem.at[k],
            recv_sem=recv_sem.at[k],
            device_id=peer,
            device_id_type=MESH,
        )
        copy.start()
        copies.append(copy)
    for copy in copies:
        copy.wait_send()
    for k in range(1, n):
        src_rank = lax.rem(me + n - k, n)
        pltpu.make_async_remote_copy(
            src_ref=src_for(_peer_coords(group, src_rank)),
            dst_ref=land.at[src_rank],
            send_sem=send_sem.at[k],
            recv_sem=recv_sem.at[k],
            device_id=_peer_coords(group, src_rank),
            device_id_type=MESH,
        ).wait_recv()
    o_ref[...] = land[...]
    own = src_for(_peer_coords(group, me))
    o_ref[me] = own[...]


def exchange(x, group, cid, select=None):
    n = 1
    for a in group:
        n *= lax.axis_size(a)
    block = x.shape if select is None else x.shape[1:]
    return pl.pallas_call(
        functools.partial(_exchange_kernel, group, n, select),
        out_shape=jax.ShapeDtypeStruct((n,) + block, x.dtype),
        in_specs=[pl.BlockSpec(memory_space=pltpu.VMEM)],
        out_specs=pl.BlockSpec(memory_space=pltpu.VMEM),
        scratch_shapes=[
            pltpu.VMEM((n,) + block, x.dtype),
            pltpu.SemaphoreType.DMA((n,)),
            pltpu.SemaphoreType.DMA((n,)),
        ],
        compiler_params=pltpu.CompilerParams(collective_id=cid, has_side_effects=True),
    )(x)


def _send_all(group, me, n, src_for, land, ssem, rsem):
    copies = []
    for k in range(1, n):
        peer = _peer_coords(group, lax.rem(me + k, n))
        copy = pltpu.make_async_remote_copy(
            src_ref=src_for(peer), dst_ref=land.at[me], send_sem=ssem.at[k],
            recv_sem=rsem.at[k], device_id=peer, device_id_type=MESH,
        )
        copy.start()
        copies.append(copy)
    return copies


def _wait_all(group, me, n, src_for, land, ssem, rsem, copies):
    for copy in copies:
        copy.wait_send()
    for k in range(1, n):
        src_rank = lax.rem(me + n - k, n)
        peer = _peer_coords(group, src_rank)
        pltpu.make_async_remote_copy(
            src_ref=src_for(peer), dst_ref=land.at[src_rank], send_sem=ssem.at[k],
            recv_sem=rsem.at[k], device_id=peer, device_id_type=MESH,
        ).wait_recv()


def _gelu(v):
    return 0.5 * v * (1.0 + jnp.tanh(0.7978845608028654 * (v + 0.044715 * v * v * v)))


def _slots_kernel(n_dp, n_seq, n_ex, tok_v, phi_ref, w_in_hbm, w_out_hbm,
                  wb_out, den_out, so_out, mx_ref, mx_land, num_ref, w_in_v, w_out_v, w_sem,
                  num_land, lg_src, lg_land, si_src, si_land, slot_in, part_src, pp_land,
                  cs_src, cs_land, so_src, so_land, sems):
    gs, gp, ge = ("seq",), ("dp",), ("expert",)
    me_s, me_p, me_e = _my_rank(gs), _my_rank(gp), _my_rank(ge)
    w_in_copy = pltpu.make_async_copy(w_in_hbm, w_in_v, w_sem.at[0])
    w_out_copy = pltpu.make_async_copy(w_out_hbm, w_out_v, w_sem.at[1])
    w_in_copy.start()
    w_out_copy.start()

    barrier = pltpu.get_barrier_semaphore()
    for group, me, n in ((gs, me_s, n_seq), (gp, me_p, n_dp), (ge, me_e, n_ex)):
        for k in range(1, n):
            peer = _peer_coords(group, lax.rem(me + k, n))
            pl.semaphore_signal(barrier, inc=1, device_id=peer, device_id_type=MESH)

    logits = lax.dot_general(
        phi_ref[...], tok_v[...], (((1,), (1,)), ((), ())), preferred_element_type=jnp.float32
    )
    mx_ref[...] = jnp.broadcast_to(jnp.max(logits, axis=1, keepdims=True), mx_ref.shape)
    rows_out = lg_src.shape[2]
    for g in range(n_ex):
        lg_src[g] = logits[:, g * rows_out:(g + 1) * rows_out]
    pl.semaphore_wait(barrier, n_seq - 1 + n_dp - 1 + n_ex - 1)

    stage_a0 = (gs, me_s, n_seq, lambda c: mx_ref, mx_land, sems.at[14], sems.at[15])
    ex_pos = AXES.index("expert")
    stage_phi = (ge, me_e, n_ex, lambda c: lg_src.at[c[ex_pos]], lg_land, sems.at[4], sems.at[5])
    started_a0 = _send_all(*stage_a0)
    started_phi = _send_all(*stage_phi)
    _wait_all(*stage_a0, started_a0)
    mx_land[me_s] = mx_ref[...]
    slot_max = jnp.max(mx_land[...], axis=0)[:, 0:1]
    spread = jnp.exp(logits - slot_max)
    denominator = jnp.sum(spread, axis=1, keepdims=True)
    d = tok_v.shape[1]
    num_ref[:, 0:d] = jnp.dot(spread.astype(jnp.bfloat16), tok_v[...], preferred_element_type=jnp.float32)
    num_ref[:, d:d + 128] = jnp.broadcast_to(denominator, (denominator.shape[0], 128))

    stage_a = (gs, me_s, n_seq, lambda c: num_ref, num_land, sems.at[0], sems.at[1])
    _wait_all(*stage_a, _send_all(*stage_a))
    num_land[me_s] = num_ref[...]

    totals = jnp.sum(num_land[...], axis=0)
    si_src[...] = (totals[:, 0:d] / totals[:, d:d + 1]).astype(si_src.dtype)

    stage_a2 = (gp, me_p, n_dp, lambda c: si_src, si_land, sems.at[6], sems.at[7])
    _wait_all(*stage_a2, _send_all(*stage_a2))
    si_land[me_p] = si_src[...]
    own_e = num_ref.shape[0]
    for c in range(n_dp):
        value = si_land[c].astype(jnp.float32)
        for e in range(own_e):
            slot_in[e, pl.ds(c, 1), :] = value[e:e + 1, :]

    w_in_copy.wait()
    w_out_copy.wait()
    for e in range(own_e):
        hidden = jnp.dot(slot_in[e].astype(jnp.bfloat16), w_in_v[e], preferred_element_type=jnp.float32)
        hidden = _gelu(hidden).astype(jnp.bfloat16)
        part = jnp.dot(hidden, w_out_v[e], preferred_element_type=jnp.float32)
        for c in range(n_dp):
            part_src[c, pl.ds(e, 1), :] = part[c:c + 1, :]

    dp_pos = AXES.index("dp")
    stage_b1 = (gp, me_p, n_dp, lambda c: part_src.at[c[dp_pos]], pp_land, sems.at[8], sems.at[9])
    _wait_all(*stage_b1, _send_all(*stage_b1))
    partner = lax.rem(me_p + 1, n_dp)
    cs_src[...] = part_src[me_p] + pp_land[partner]

    stage_b2 = (gs, me_s, n_seq, lambda c: cs_src, cs_land, sems.at[10], sems.at[11])
    _wait_all(*stage_b2, _send_all(*stage_b2))
    cs_land[me_s] = cs_src[...]
    so_src[...] = jnp.sum(cs_land[...], axis=0).astype(so_src.dtype)

    stage_c = (ge, me_e, n_ex, lambda c: so_src, so_land, sems.at[12], sems.at[13])
    started_c = _send_all(*stage_c)
    _wait_all(*stage_phi, started_phi)
    lg_land[me_e] = lg_src[me_e]
    row_logits = lg_land[...]
    row_max = jnp.max(jnp.max(row_logits, axis=0), axis=0, keepdims=True)
    weights = jnp.exp(row_logits - row_max[None])
    wb_out[...] = weights.astype(wb_out.dtype)
    den_out[...] = jnp.sum(jnp.sum(weights, axis=0), axis=0, keepdims=True)
    _wait_all(*stage_c, started_c)
    so_land[me_e] = so_src[...]
    so_out[...] = so_land[...]


def expert_slots(tokens, phi_t, w_in, w_out, cid):
    n_dp, n_seq, n_ex = (lax.axis_size(a) for a in AXES)
    own_e, d = phi_t.shape
    vmem = pl.BlockSpec(memory_space=pltpu.VMEM)
    anywhere = pl.BlockSpec(memory_space=pl.ANY)
    gathered = jax.ShapeDtypeStruct((n_ex, own_e, d), jnp.bfloat16)
    rows_out = tokens.shape[0] // n_ex
    weights = jax.ShapeDtypeStruct((n_ex, own_e, rows_out), jnp.bfloat16)
    totals = jax.ShapeDtypeStruct((1, rows_out), jnp.float32)
    return pl.pallas_call(
        functools.partial(_slots_kernel, n_dp, n_seq, n_ex),
        out_shape=(weights, totals, gathered),
        in_specs=[vmem, vmem, anywhere, anywhere],
        out_specs=(vmem, vmem, vmem),
        scratch_shapes=[
            pltpu.VMEM((own_e, 128), jnp.float32),
            pltpu.VMEM((n_seq, own_e, 128), jnp.float32),
            pltpu.VMEM((own_e, d + 128), jnp.float32),
            pltpu.VMEM(w_in.shape, w_in.dtype),
            pltpu.VMEM(w_out.shape, w_out.dtype),
            pltpu.SemaphoreType.DMA((2,)),
            pltpu.VMEM((n_seq, own_e, d + 128), jnp.float32),
            pltpu.VMEM((n_ex, own_e, rows_out), jnp.float32),
            pltpu.VMEM((n_ex, own_e, rows_out), jnp.float32),
            pltpu.VMEM((own_e, d), jnp.bfloat16),
            pltpu.VMEM((n_dp, own_e, d), jnp.bfloat16),
            pltpu.VMEM((own_e, n_dp, d), jnp.float32),
            pltpu.VMEM((n_dp, own_e, d), jnp.float32),
            pltpu.VMEM((n_dp, own_e, d), jnp.float32),
            pltpu.VMEM((own_e, d), jnp.float32),
            pltpu.VMEM((n_seq, own_e, d), jnp.float32),
            pltpu.VMEM((own_e, d), jnp.bfloat16),
            pltpu.VMEM((n_ex, own_e, d), jnp.bfloat16),
            pltpu.SemaphoreType.DMA((16, max(n_dp, n_seq, n_ex))),
        ],
        compiler_params=pltpu.CompilerParams(
            collective_id=cid, has_side_effects=True, vmem_limit_bytes=48 * 1024 * 1024
        ),
    )(tokens, phi_t, w_in, w_out)

def on_device(tokens, phi, w_in, w_out):
    n_expert = lax.axis_size("expert")
    n_dp = lax.axis_size("dp")
    n_seq = lax.axis_size("seq")
    own_e = phi.shape[1]
    d = tokens.shape[1]
    rows_out = tokens.shape[0] // n_expert
    weight_g, total, slot_g = expert_slots(tokens, phi.T, w_in, w_out, 1)
    combine_weights = weight_g.reshape(n_expert * own_e, rows_out)
    slot_out = slot_g.reshape(n_expert * own_e, d)
    mixed_numer = lax.dot_general(
        combine_weights,
        slot_out,
        (((0,), (0,)), ((), ())),
        preferred_element_type=jnp.float32,
    )
    return (mixed_numer / total[0][:, None]).astype(jnp.bfloat16)


def solution(mesh):
    placed = (
        P(("dp", "seq"), None),
        P(None, "expert"),
        P("expert", None, ("dp", "seq")),
        P("expert", ("dp", "seq"), None),
    )
    return jax.shard_map(
        on_device,
        mesh=mesh,
        in_specs=placed,
        out_specs=P(("dp", "seq", "expert"), None),
        check_vma=False,
    )
```

```python
import functools

import jax
import jax.numpy as jnp
from jax import lax
from jax.experimental import pallas as pl
from jax.experimental.pallas import tpu as pltpu
from jax.sharding import PartitionSpec as P

MESH = pl.DeviceIdType.MESH
AXES = ("dp", "seq", "expert")


def _peer_coords(group, rank):
    coords = {a: lax.axis_index(a) for a in AXES}
    sizes = [lax.axis_size(a) for a in group]
    rest = rank
    for a, s in reversed(list(zip(group, sizes))):
        coords[a] = lax.rem(rest, s)
        rest = rest // s
    return tuple(coords[a] for a in AXES)


def _my_rank(group):
    rank = 0
    for a in group:
        rank = rank * lax.axis_size(a) + lax.axis_index(a)
    return rank


def _exchange_kernel(group, n, select, x_ref, o_ref, land, send_sem, recv_sem):
    me = _my_rank(group)
    barrier = pltpu.get_barrier_semaphore()
    for k in range(1, n):
        peer = _peer_coords(group, lax.rem(me + k, n))
        pl.semaphore_signal(barrier, inc=1, device_id=peer, device_id_type=MESH)
    pl.semaphore_wait(barrier, n - 1)

    def src_for(coords):
        if select is None:
            return x_ref
        return x_ref.at[coords[AXES.index(select)]]

    copies = []
    for k in range(1, n):
        peer = _peer_coords(group, lax.rem(me + k, n))
        copy = pltpu.make_async_remote_copy(
            src_ref=src_for(peer),
            dst_ref=land.at[me],
            send_sem=send_sem.at[k],
            recv_sem=recv_sem.at[k],
            device_id=peer,
            device_id_type=MESH,
        )
        copy.start()
        copies.append(copy)
    for copy in copies:
        copy.wait_send()
    for k in range(1, n):
        src_rank = lax.rem(me + n - k, n)
        pltpu.make_async_remote_copy(
            src_ref=src_for(_peer_coords(group, src_rank)),
            dst_ref=land.at[src_rank],
            send_sem=send_sem.at[k],
            recv_sem=recv_sem.at[k],
            device_id=_peer_coords(group, src_rank),
            device_id_type=MESH,
        ).wait_recv()
    o_ref[...] = land[...]
    own = src_for(_peer_coords(group, me))
    o_ref[me] = own[...]


def exchange(x, group, cid, select=None):
    n = 1
    for a in group:
        n *= lax.axis_size(a)
    block = x.shape if select is None else x.shape[1:]
    return pl.pallas_call(
        functools.partial(_exchange_kernel, group, n, select),
        out_shape=jax.ShapeDtypeStruct((n,) + block, x.dtype),
        in_specs=[pl.BlockSpec(memory_space=pltpu.VMEM)],
        out_specs=pl.BlockSpec(memory_space=pltpu.VMEM),
        scratch_shapes=[
            pltpu.VMEM((n,) + block, x.dtype),
            pltpu.SemaphoreType.DMA((n,)),
            pltpu.SemaphoreType.DMA((n,)),
        ],
        compiler_params=pltpu.CompilerParams(collective_id=cid, has_side_effects=True),
    )(x)


def _send_all(group, me, n, src_for, land, ssem, rsem):
    copies = []
    for k in range(1, n):
        peer = _peer_coords(group, lax.rem(me + k, n))
        copy = pltpu.make_async_remote_copy(
            src_ref=src_for(peer), dst_ref=land.at[me], send_sem=ssem.at[k],
            recv_sem=rsem.at[k], device_id=peer, device_id_type=MESH,
        )
        copy.start()
        copies.append(copy)
    return copies


def _wait_all(group, me, n, src_for, land, ssem, rsem, copies):
    for copy in copies:
        copy.wait_send()
    for k in range(1, n):
        src_rank = lax.rem(me + n - k, n)
        peer = _peer_coords(group, src_rank)
        pltpu.make_async_remote_copy(
            src_ref=src_for(peer), dst_ref=land.at[src_rank], send_sem=ssem.at[k],
            recv_sem=rsem.at[k], device_id=peer, device_id_type=MESH,
        ).wait_recv()


def _gelu(v):
    return 0.5 * v * (1.0 + jnp.tanh(0.7978845608028654 * (v + 0.044715 * v * v * v)))


def _slots_kernel(n_dp, n_seq, n_ex, tok_v, phi_ref, w_in_hbm, w_out_hbm,
                  wb_out, den_out, so_out, mx_ref, mx_land, num_ref, w_in_v, w_out_v, w_sem,
                  num_land, lg_src, lg_land, si_src, si_land, slot_in, part_src, pp_land,
                  cs_src, cs_land, so_src, so_land, sems, b1_sems, b2_sems):
    gs, gp, ge = ("seq",), ("dp",), ("expert",)
    me_s, me_p, me_e = _my_rank(gs), _my_rank(gp), _my_rank(ge)
    w_in_copy = pltpu.make_async_copy(w_in_hbm, w_in_v, w_sem.at[0])
    w_out_copy = pltpu.make_async_copy(w_out_hbm, w_out_v, w_sem.at[1])
    w_in_copy.start()
    w_out_copy.start()

    barrier = pltpu.get_barrier_semaphore()
    for group, me, n in ((gs, me_s, n_seq), (gp, me_p, n_dp), (ge, me_e, n_ex)):
        for k in range(1, n):
            peer = _peer_coords(group, lax.rem(me + k, n))
            pl.semaphore_signal(barrier, inc=1, device_id=peer, device_id_type=MESH)

    logits = lax.dot_general(
        phi_ref[...], tok_v[...], (((1,), (1,)), ((), ())), preferred_element_type=jnp.float32
    )
    mx_ref[...] = jnp.broadcast_to(jnp.max(logits, axis=1, keepdims=True), mx_ref.shape)
    rows_out = lg_src.shape[2]
    for g in range(n_ex):
        lg_src[g] = logits[:, g * rows_out:(g + 1) * rows_out]
    pl.semaphore_wait(barrier, n_seq - 1 + n_dp - 1 + n_ex - 1)

    stage_a0 = (gs, me_s, n_seq, lambda c: mx_ref, mx_land, sems.at[14], sems.at[15])
    ex_pos = AXES.index("expert")
    stage_phi = (ge, me_e, n_ex, lambda c: lg_src.at[c[ex_pos]], lg_land, sems.at[4], sems.at[5])
    started_a0 = _send_all(*stage_a0)
    started_phi = _send_all(*stage_phi)
    _wait_all(*stage_a0, started_a0)
    mx_land[me_s] = mx_ref[...]
    slot_max = jnp.max(mx_land[...], axis=0)[:, 0:1]
    spread = jnp.exp(logits - slot_max)
    denominator = jnp.sum(spread, axis=1, keepdims=True)
    d = tok_v.shape[1]
    num_ref[:, 0:d] = jnp.dot(spread.astype(jnp.bfloat16), tok_v[...], preferred_element_type=jnp.float32)
    num_ref[:, d:d + 128] = jnp.broadcast_to(denominator, (denominator.shape[0], 128))

    stage_a = (gs, me_s, n_seq, lambda c: num_ref, num_land, sems.at[0], sems.at[1])
    _wait_all(*stage_a, _send_all(*stage_a))
    num_land[me_s] = num_ref[...]

    totals = jnp.sum(num_land[...], axis=0)
    si_src[...] = (totals[:, 0:d] / totals[:, d:d + 1]).astype(si_src.dtype)

    stage_a2 = (gp, me_p, n_dp, lambda c: si_src, si_land, sems.at[6], sems.at[7])
    _wait_all(*stage_a2, _send_all(*stage_a2))
    si_land[me_p] = si_src[...]
    own_e = num_ref.shape[0]
    for c in range(n_dp):
        value = si_land[c].astype(jnp.float32)
        for e in range(own_e):
            slot_in[e, pl.ds(c, 1), :] = value[e:e + 1, :]

    w_in_copy.wait()
    w_out_copy.wait()
    partner = lax.rem(me_p + 1, n_dp)
    partner_dev = _peer_coords(gp, partner)
    seq_peers = [_peer_coords(gs, lax.rem(me_s + j, n_seq)) for j in range(1, n_seq)]
    seq_srcs = [lax.rem(me_s + n_seq - j, n_seq) for j in range(1, n_seq)]
    b1 = []
    for e in range(own_e):
        hidden = jnp.dot(slot_in[e].astype(jnp.bfloat16), w_in_v[e], preferred_element_type=jnp.float32)
        hidden = _gelu(hidden).astype(jnp.bfloat16)
        part_src[e] = jnp.dot(hidden, w_out_v[e], preferred_element_type=jnp.float32)
        copy = pltpu.make_async_remote_copy(
            src_ref=part_src.at[e], dst_ref=pp_land.at[e], send_sem=b1_sems.at[e, 0],
            recv_sem=b1_sems.at[e, 1], device_id=partner_dev, device_id_type=MESH,
        )
        copy.start()
        b1.append(copy)
    b2 = []
    for e in range(own_e):
        b1[e].wait_send()
        b1[e].wait_recv()
        cs_src[e] = part_src[e, pl.ds(me_p, 1), :] + pp_land[e, pl.ds(me_p, 1), :]
        for j in range(1, n_seq):
            copy = pltpu.make_async_remote_copy(
                src_ref=cs_src.at[e], dst_ref=cs_land.at[me_s, e], send_sem=b2_sems.at[e, 0, j],
                recv_sem=b2_sems.at[e, 1, j], device_id=seq_peers[j - 1], device_id_type=MESH,
            )
            copy.start()
            b2.append(copy)
    for copy in b2:
        copy.wait_send()
    for e in range(own_e):
        for j in range(1, n_seq):
            pltpu.make_async_remote_copy(
                src_ref=cs_src.at[e], dst_ref=cs_land.at[seq_srcs[j - 1], e],
                send_sem=b2_sems.at[e, 0, j], recv_sem=b2_sems.at[e, 1, j],
                device_id=_peer_coords(gs, seq_srcs[j - 1]), device_id_type=MESH,
            ).wait_recv()
    cs_land[me_s] = cs_src[...]
    total = jnp.sum(cs_land[...], axis=0)
    so_src[...] = jnp.concatenate([total[e] for e in range(own_e)], axis=0).astype(so_src.dtype)

    stage_c = (ge, me_e, n_ex, lambda c: so_src, so_land, sems.at[12], sems.at[13])
    started_c = _send_all(*stage_c)
    _wait_all(*stage_phi, started_phi)
    lg_land[me_e] = lg_src[me_e]
    row_logits = lg_land[...]
    row_max = jnp.max(jnp.max(row_logits, axis=0), axis=0, keepdims=True)
    weights = jnp.exp(row_logits - row_max[None])
    wb_out[...] = weights.astype(wb_out.dtype)
    den_out[...] = jnp.sum(jnp.sum(weights, axis=0), axis=0, keepdims=True)
    _wait_all(*stage_c, started_c)
    so_land[me_e] = so_src[...]
    so_out[...] = so_land[...]


def expert_slots(tokens, phi_t, w_in, w_out, cid):
    n_dp, n_seq, n_ex = (lax.axis_size(a) for a in AXES)
    own_e, d = phi_t.shape
    vmem = pl.BlockSpec(memory_space=pltpu.VMEM)
    anywhere = pl.BlockSpec(memory_space=pl.ANY)
    gathered = jax.ShapeDtypeStruct((n_ex, own_e, d), jnp.bfloat16)
    rows_out = tokens.shape[0] // n_ex
    weights = jax.ShapeDtypeStruct((n_ex, own_e, rows_out), jnp.bfloat16)
    totals = jax.ShapeDtypeStruct((1, rows_out), jnp.float32)
    return pl.pallas_call(
        functools.partial(_slots_kernel, n_dp, n_seq, n_ex),
        out_shape=(weights, totals, gathered),
        in_specs=[vmem, vmem, anywhere, anywhere],
        out_specs=(vmem, vmem, vmem),
        scratch_shapes=[
            pltpu.VMEM((own_e, 128), jnp.float32),
            pltpu.VMEM((n_seq, own_e, 128), jnp.float32),
            pltpu.VMEM((own_e, d + 128), jnp.float32),
            pltpu.VMEM(w_in.shape, w_in.dtype),
            pltpu.VMEM(w_out.shape, w_out.dtype),
            pltpu.SemaphoreType.DMA((2,)),
            pltpu.VMEM((n_seq, own_e, d + 128), jnp.float32),
            pltpu.VMEM((n_ex, own_e, rows_out), jnp.float32),
            pltpu.VMEM((n_ex, own_e, rows_out), jnp.float32),
            pltpu.VMEM((own_e, d), jnp.bfloat16),
            pltpu.VMEM((n_dp, own_e, d), jnp.bfloat16),
            pltpu.VMEM((own_e, n_dp, d), jnp.float32),
            pltpu.VMEM((own_e, n_dp, d), jnp.float32),
            pltpu.VMEM((own_e, n_dp, d), jnp.float32),
            pltpu.VMEM((own_e, 1, d), jnp.float32),
            pltpu.VMEM((n_seq, own_e, 1, d), jnp.float32),
            pltpu.VMEM((own_e, d), jnp.bfloat16),
            pltpu.VMEM((n_ex, own_e, d), jnp.bfloat16),
            pltpu.SemaphoreType.DMA((16, max(n_dp, n_seq, n_ex))),
            pltpu.SemaphoreType.DMA((own_e, 2)),
            pltpu.SemaphoreType.DMA((own_e, 2, n_seq)),
        ],
        compiler_params=pltpu.CompilerParams(
            collective_id=cid, has_side_effects=True, vmem_limit_bytes=48 * 1024 * 1024
        ),
    )(tokens, phi_t, w_in, w_out)

def on_device(tokens, phi, w_in, w_out):
    n_expert = lax.axis_size("expert")
    n_dp = lax.axis_size("dp")
    n_seq = lax.axis_size("seq")
    own_e = phi.shape[1]
    d = tokens.shape[1]
    rows_out = tokens.shape[0] // n_expert
    weight_g, total, slot_g = expert_slots(tokens, phi.T, w_in, w_out, 1)
    combine_weights = weight_g.reshape(n_expert * own_e, rows_out)
    slot_out = slot_g.reshape(n_expert * own_e, d)
    mixed_numer = lax.dot_general(
        combine_weights,
        slot_out,
        (((0,), (0,)), ((), ())),
        preferred_element_type=jnp.float32,
    )
    return (mixed_numer / total[0][:, None]).astype(jnp.bfloat16)


def solution(mesh):
    placed = (
        P(("dp", "seq"), None),
        P(None, "expert"),
        P("expert", None, ("dp", "seq")),
        P("expert", ("dp", "seq"), None),
    )
    return jax.shard_map(
        on_device,
        mesh=mesh,
        in_specs=placed,
        out_specs=P(("dp", "seq", "expert"), None),
        check_vma=False,
    )
```

```python
import functools

import jax
import jax.numpy as jnp
from jax import lax
from jax.experimental import pallas as pl
from jax.experimental.pallas import tpu as pltpu
from jax.sharding import PartitionSpec as P

MESH = pl.DeviceIdType.MESH
AXES = ("dp", "seq", "expert")


def _peer_coords(group, rank):
    coords = {a: lax.axis_index(a) for a in AXES}
    sizes = [lax.axis_size(a) for a in group]
    rest = rank
    for a, s in reversed(list(zip(group, sizes))):
        coords[a] = lax.rem(rest, s)
        rest = rest // s
    return tuple(coords[a] for a in AXES)


def _my_rank(group):
    rank = 0
    for a in group:
        rank = rank * lax.axis_size(a) + lax.axis_index(a)
    return rank


def _exchange_kernel(group, n, select, x_ref, o_ref, land, send_sem, recv_sem):
    me = _my_rank(group)
    barrier = pltpu.get_barrier_semaphore()
    for k in range(1, n):
        peer = _peer_coords(group, lax.rem(me + k, n))
        pl.semaphore_signal(barrier, inc=1, device_id=peer, device_id_type=MESH)
    pl.semaphore_wait(barrier, n - 1)

    def src_for(coords):
        if select is None:
            return x_ref
        return x_ref.at[coords[AXES.index(select)]]

    copies = []
    for k in range(1, n):
        peer = _peer_coords(group, lax.rem(me + k, n))
        copy = pltpu.make_async_remote_copy(
            src_ref=src_for(peer),
            dst_ref=land.at[me],
            send_sem=send_sem.at[k],
            recv_sem=recv_sem.at[k],
            device_id=peer,
            device_id_type=MESH,
        )
        copy.start()
        copies.append(copy)
    for copy in copies:
        copy.wait_send()
    for k in range(1, n):
        src_rank = lax.rem(me + n - k, n)
        pltpu.make_async_remote_copy(
            src_ref=src_for(_peer_coords(group, src_rank)),
            dst_ref=land.at[src_rank],
            send_sem=send_sem.at[k],
            recv_sem=recv_sem.at[k],
            device_id=_peer_coords(group, src_rank),
            device_id_type=MESH,
        ).wait_recv()
    o_ref[...] = land[...]
    own = src_for(_peer_coords(group, me))
    o_ref[me] = own[...]


def exchange(x, group, cid, select=None):
    n = 1
    for a in group:
        n *= lax.axis_size(a)
    block = x.shape if select is None else x.shape[1:]
    return pl.pallas_call(
        functools.partial(_exchange_kernel, group, n, select),
        out_shape=jax.ShapeDtypeStruct((n,) + block, x.dtype),
        in_specs=[pl.BlockSpec(memory_space=pltpu.VMEM)],
        out_specs=pl.BlockSpec(memory_space=pltpu.VMEM),
        scratch_shapes=[
            pltpu.VMEM((n,) + block, x.dtype),
            pltpu.SemaphoreType.DMA((n,)),
            pltpu.SemaphoreType.DMA((n,)),
        ],
        compiler_params=pltpu.CompilerParams(collective_id=cid, has_side_effects=True),
    )(x)


def _issue_order(group, n):
    if group == ("seq",):
        return sorted(range(1, n), key=lambda k: -min(k, n - k))
    return list(range(1, n))


def _send_all(group, me, n, src_for, land, ssem, rsem):
    copies = []
    for k in _issue_order(group, n):
        peer = _peer_coords(group, lax.rem(me + k, n))
        copy = pltpu.make_async_remote_copy(
            src_ref=src_for(peer), dst_ref=land.at[me], send_sem=ssem.at[k],
            recv_sem=rsem.at[k], device_id=peer, device_id_type=MESH,
        )
        copy.start()
        copies.append(copy)
    return copies


def _wait_all(group, me, n, src_for, land, ssem, rsem, copies):
    for copy in copies:
        copy.wait_send()
    for k in range(1, n):
        src_rank = lax.rem(me + n - k, n)
        peer = _peer_coords(group, src_rank)
        pltpu.make_async_remote_copy(
            src_ref=src_for(peer), dst_ref=land.at[src_rank], send_sem=ssem.at[k],
            recv_sem=rsem.at[k], device_id=peer, device_id_type=MESH,
        ).wait_recv()


def _gelu(v):
    return 0.5 * v * (1.0 + jnp.tanh(0.7978845608028654 * (v + 0.044715 * v * v * v)))


def _slots_kernel(n_dp, n_seq, n_ex, tok_v, phi_ref, w_in_hbm, w_out_hbm,
                  wb_out, den_out, so_out, mx_ref, mx_land, num_ref, w_in_v, w_out_v, w_sem,
                  num_land, lg_src, lg_land, si_src, si_land, slot_in, part_src, pp_land,
                  cs_src, cs_land, so_src, so_land, sems):
    gs, gp, ge = ("seq",), ("dp",), ("expert",)
    me_s, me_p, me_e = _my_rank(gs), _my_rank(gp), _my_rank(ge)
    w_in_copy = pltpu.make_async_copy(w_in_hbm, w_in_v, w_sem.at[0])
    w_out_copy = pltpu.make_async_copy(w_out_hbm, w_out_v, w_sem.at[1])
    w_in_copy.start()
    w_out_copy.start()

    barrier = pltpu.get_barrier_semaphore()
    for group, me, n in ((gs, me_s, n_seq), (gp, me_p, n_dp), (ge, me_e, n_ex)):
        for k in _issue_order(group, n):
            peer = _peer_coords(group, lax.rem(me + k, n))
            pl.semaphore_signal(barrier, inc=1, device_id=peer, device_id_type=MESH)

    logits = lax.dot_general(
        phi_ref[...], tok_v[...], (((1,), (1,)), ((), ())), preferred_element_type=jnp.float32
    )
    mx_ref[...] = jnp.broadcast_to(jnp.max(logits, axis=1, keepdims=True), mx_ref.shape)
    rows_out = lg_src.shape[2]
    for g in range(n_ex):
        lg_src[g] = logits[:, g * rows_out:(g + 1) * rows_out]
    pl.semaphore_wait(barrier, n_seq - 1 + n_dp - 1 + n_ex - 1)

    stage_a0 = (gs, me_s, n_seq, lambda c: mx_ref, mx_land, sems.at[14], sems.at[15])
    ex_pos = AXES.index("expert")
    stage_phi = (ge, me_e, n_ex, lambda c: lg_src.at[c[ex_pos]], lg_land, sems.at[4], sems.at[5])
    started_a0 = _send_all(*stage_a0)
    started_phi = _send_all(*stage_phi)
    _wait_all(*stage_a0, started_a0)
    mx_land[me_s] = mx_ref[...]
    slot_max = jnp.max(mx_land[...], axis=0)[:, 0:1]
    spread = jnp.exp(logits - slot_max)
    denominator = jnp.sum(spread, axis=1, keepdims=True)
    d = tok_v.shape[1]
    num_ref[:, 0:d] = jnp.dot(spread.astype(jnp.bfloat16), tok_v[...], preferred_element_type=jnp.float32)
    num_ref[:, d:d + 128] = jnp.broadcast_to(denominator, (denominator.shape[0], 128))

    stage_a = (gs, me_s, n_seq, lambda c: num_ref, num_land, sems.at[0], sems.at[1])
    _wait_all(*stage_a, _send_all(*stage_a))
    num_land[me_s] = num_ref[...]

    totals = jnp.sum(num_land[...], axis=0)
    si_src[...] = (totals[:, 0:d] / totals[:, d:d + 1]).astype(si_src.dtype)

    stage_a2 = (gp, me_p, n_dp, lambda c: si_src, si_land, sems.at[6], sems.at[7])
    _wait_all(*stage_a2, _send_all(*stage_a2))
    si_land[me_p] = si_src[...]
    own_e = num_ref.shape[0]
    for c in range(n_dp):
        value = si_land[c].astype(jnp.float32)
        for e in range(own_e):
            slot_in[e, pl.ds(c, 1), :] = value[e:e + 1, :]

    w_in_copy.wait()
    w_out_copy.wait()
    for e in range(own_e):
        hidden = jnp.dot(slot_in[e].astype(jnp.bfloat16), w_in_v[e], preferred_element_type=jnp.float32)
        hidden = _gelu(hidden).astype(jnp.bfloat16)
        part = jnp.dot(hidden, w_out_v[e], preferred_element_type=jnp.float32)
        for c in range(n_dp):
            part_src[c, pl.ds(e, 1), :] = part[c:c + 1, :]

    dp_pos = AXES.index("dp")
    stage_b1 = (gp, me_p, n_dp, lambda c: part_src.at[c[dp_pos]], pp_land, sems.at[8], sems.at[9])
    _wait_all(*stage_b1, _send_all(*stage_b1))
    partner = lax.rem(me_p + 1, n_dp)
    cs_src[...] = part_src[me_p] + pp_land[partner]

    stage_b2 = (gs, me_s, n_seq, lambda c: cs_src, cs_land, sems.at[10], sems.at[11])
    _wait_all(*stage_b2, _send_all(*stage_b2))
    cs_land[me_s] = cs_src[...]
    so_src[...] = jnp.sum(cs_land[...], axis=0).astype(so_src.dtype)

    stage_c = (ge, me_e, n_ex, lambda c: so_src, so_land, sems.at[12], sems.at[13])
    started_c = _send_all(*stage_c)
    _wait_all(*stage_phi, started_phi)
    lg_land[me_e] = lg_src[me_e]
    row_logits = lg_land[...]
    row_max = jnp.max(jnp.max(row_logits, axis=0), axis=0, keepdims=True)
    weights = jnp.exp(row_logits - row_max[None])
    wb_out[...] = weights.astype(wb_out.dtype)
    den_out[...] = jnp.sum(jnp.sum(weights, axis=0), axis=0, keepdims=True)
    _wait_all(*stage_c, started_c)
    so_land[me_e] = so_src[...]
    so_out[...] = so_land[...]


def expert_slots(tokens, phi_t, w_in, w_out, cid):
    n_dp, n_seq, n_ex = (lax.axis_size(a) for a in AXES)
    own_e, d = phi_t.shape
    vmem = pl.BlockSpec(memory_space=pltpu.VMEM)
    anywhere = pl.BlockSpec(memory_space=pl.ANY)
    gathered = jax.ShapeDtypeStruct((n_ex, own_e, d), jnp.bfloat16)
    rows_out = tokens.shape[0] // n_ex
    weights = jax.ShapeDtypeStruct((n_ex, own_e, rows_out), jnp.bfloat16)
    totals = jax.ShapeDtypeStruct((1, rows_out), jnp.float32)
    return pl.pallas_call(
        functools.partial(_slots_kernel, n_dp, n_seq, n_ex),
        out_shape=(weights, totals, gathered),
        in_specs=[vmem, vmem, anywhere, anywhere],
        out_specs=(vmem, vmem, vmem),
        scratch_shapes=[
            pltpu.VMEM((own_e, 128), jnp.float32),
            pltpu.VMEM((n_seq, own_e, 128), jnp.float32),
            pltpu.VMEM((own_e, d + 128), jnp.float32),
            pltpu.VMEM(w_in.shape, w_in.dtype),
            pltpu.VMEM(w_out.shape, w_out.dtype),
            pltpu.SemaphoreType.DMA((2,)),
            pltpu.VMEM((n_seq, own_e, d + 128), jnp.float32),
            pltpu.VMEM((n_ex, own_e, rows_out), jnp.float32),
            pltpu.VMEM((n_ex, own_e, rows_out), jnp.float32),
            pltpu.VMEM((own_e, d), jnp.bfloat16),
            pltpu.VMEM((n_dp, own_e, d), jnp.bfloat16),
            pltpu.VMEM((own_e, n_dp, d), jnp.float32),
            pltpu.VMEM((n_dp, own_e, d), jnp.float32),
            pltpu.VMEM((n_dp, own_e, d), jnp.float32),
            pltpu.VMEM((own_e, d), jnp.float32),
            pltpu.VMEM((n_seq, own_e, d), jnp.float32),
            pltpu.VMEM((own_e, d), jnp.bfloat16),
            pltpu.VMEM((n_ex, own_e, d), jnp.bfloat16),
            pltpu.SemaphoreType.DMA((16, max(n_dp, n_seq, n_ex))),
        ],
        compiler_params=pltpu.CompilerParams(
            collective_id=cid, has_side_effects=True, vmem_limit_bytes=48 * 1024 * 1024
        ),
    )(tokens, phi_t, w_in, w_out)

def on_device(tokens, phi, w_in, w_out):
    n_expert = lax.axis_size("expert")
    n_dp = lax.axis_size("dp")
    n_seq = lax.axis_size("seq")
    own_e = phi.shape[1]
    d = tokens.shape[1]
    rows_out = tokens.shape[0] // n_expert
    weight_g, total, slot_g = expert_slots(tokens, phi.T, w_in, w_out, 1)
    combine_weights = weight_g.reshape(n_expert * own_e, rows_out)
    slot_out = slot_g.reshape(n_expert * own_e, d)
    mixed_numer = lax.dot_general(
        combine_weights,
        slot_out,
        (((0,), (0,)), ((), ())),
        preferred_element_type=jnp.float32,
    )
    return (mixed_numer / total[0][:, None]).astype(jnp.bfloat16)


def solution(mesh):
    placed = (
        P(("dp", "seq"), None),
        P(None, "expert"),
        P("expert", None, ("dp", "seq")),
        P("expert", ("dp", "seq"), None),
    )
    return jax.shard_map(
        on_device,
        mesh=mesh,
        in_specs=placed,
        out_specs=P(("dp", "seq", "expert"), None),
        check_vma=False,
    )
```

```python
import functools

import jax
import jax.numpy as jnp
from jax import lax
from jax.experimental import pallas as pl
from jax.experimental.pallas import tpu as pltpu
from jax.sharding import PartitionSpec as P

MESH = pl.DeviceIdType.MESH
AXES = ("dp", "seq", "expert")


def _peer_coords(group, rank):
    coords = {a: lax.axis_index(a) for a in AXES}
    sizes = [lax.axis_size(a) for a in group]
    rest = rank
    for a, s in reversed(list(zip(group, sizes))):
        coords[a] = lax.rem(rest, s)
        rest = rest // s
    return tuple(coords[a] for a in AXES)


def _my_rank(group):
    rank = 0
    for a in group:
        rank = rank * lax.axis_size(a) + lax.axis_index(a)
    return rank


def _exchange_kernel(group, n, select, x_ref, o_ref, land, send_sem, recv_sem):
    me = _my_rank(group)
    barrier = pltpu.get_barrier_semaphore()
    for k in range(1, n):
        peer = _peer_coords(group, lax.rem(me + k, n))
        pl.semaphore_signal(barrier, inc=1, device_id=peer, device_id_type=MESH)
    pl.semaphore_wait(barrier, n - 1)

    def src_for(coords):
        if select is None:
            return x_ref
        return x_ref.at[coords[AXES.index(select)]]

    copies = []
    for k in range(1, n):
        peer = _peer_coords(group, lax.rem(me + k, n))
        copy = pltpu.make_async_remote_copy(
            src_ref=src_for(peer),
            dst_ref=land.at[me],
            send_sem=send_sem.at[k],
            recv_sem=recv_sem.at[k],
            device_id=peer,
            device_id_type=MESH,
        )
        copy.start()
        copies.append(copy)
    for copy in copies:
        copy.wait_send()
    for k in range(1, n):
        src_rank = lax.rem(me + n - k, n)
        pltpu.make_async_remote_copy(
            src_ref=src_for(_peer_coords(group, src_rank)),
            dst_ref=land.at[src_rank],
            send_sem=send_sem.at[k],
            recv_sem=recv_sem.at[k],
            device_id=_peer_coords(group, src_rank),
            device_id_type=MESH,
        ).wait_recv()
    o_ref[...] = land[...]
    own = src_for(_peer_coords(group, me))
    o_ref[me] = own[...]


def exchange(x, group, cid, select=None):
    n = 1
    for a in group:
        n *= lax.axis_size(a)
    block = x.shape if select is None else x.shape[1:]
    return pl.pallas_call(
        functools.partial(_exchange_kernel, group, n, select),
        out_shape=jax.ShapeDtypeStruct((n,) + block, x.dtype),
        in_specs=[pl.BlockSpec(memory_space=pltpu.VMEM)],
        out_specs=pl.BlockSpec(memory_space=pltpu.VMEM),
        scratch_shapes=[
            pltpu.VMEM((n,) + block, x.dtype),
            pltpu.SemaphoreType.DMA((n,)),
            pltpu.SemaphoreType.DMA((n,)),
        ],
        compiler_params=pltpu.CompilerParams(collective_id=cid, has_side_effects=True),
    )(x)


def _grid(group, n):
    side = int(round(n ** 0.5))
    if group == ("expert",) and side * side == n:
        return side
    return None


def _issue_order(group, n):
    side = _grid(group, n)
    if side is None:
        if group == ("seq",):
            return sorted(range(1, n), key=lambda k: -min(k, n - k))
        return list(range(1, n))
    ring = lambda v: min(v, side - v)
    return sorted(range(1, n), key=lambda k: -(ring(k // side) + ring(k % side)))


def _offset_rank(group, n, me, k, sign):
    side = _grid(group, n)
    if side is None:
        return lax.rem(me + sign * k + n, n)
    row = lax.rem(me // side + sign * (k // side) + side, side)
    col = lax.rem(lax.rem(me, side) + sign * (k % side) + side, side)
    return row * side + col


def _send_all(group, me, n, src_for, land, ssem, rsem):
    copies = []
    for k in _issue_order(group, n):
        peer = _peer_coords(group, _offset_rank(group, n, me, k, 1))
        copy = pltpu.make_async_remote_copy(
            src_ref=src_for(peer), dst_ref=land.at[me], send_sem=ssem.at[k],
            recv_sem=rsem.at[k], device_id=peer, device_id_type=MESH,
        )
        copy.start()
        copies.append(copy)
    return copies


def _wait_all(group, me, n, src_for, land, ssem, rsem, copies):
    for copy in copies:
        copy.wait_send()
    for k in range(1, n):
        src_rank = _offset_rank(group, n, me, k, -1)
        peer = _peer_coords(group, src_rank)
        pltpu.make_async_remote_copy(
            src_ref=src_for(peer), dst_ref=land.at[src_rank], send_sem=ssem.at[k],
            recv_sem=rsem.at[k], device_id=peer, device_id_type=MESH,
        ).wait_recv()


def _gelu(v):
    return 0.5 * v * (1.0 + jnp.tanh(0.7978845608028654 * (v + 0.044715 * v * v * v)))


def _slots_kernel(n_dp, n_seq, n_ex, tok_v, phi_ref, w_in_hbm, w_out_hbm,
                  wb_out, den_out, so_out, mx_ref, mx_land, num_ref, w_in_v, w_out_v, w_sem,
                  num_land, lg_src, lg_land, si_src, si_land, slot_in, part_src, pp_land,
                  cs_src, cs_land, so_src, so_land, sems):
    gs, gp, ge = ("seq",), ("dp",), ("expert",)
    me_s, me_p, me_e = _my_rank(gs), _my_rank(gp), _my_rank(ge)
    w_in_copy = pltpu.make_async_copy(w_in_hbm, w_in_v, w_sem.at[0])
    w_out_copy = pltpu.make_async_copy(w_out_hbm, w_out_v, w_sem.at[1])
    w_in_copy.start()
    w_out_copy.start()

    barrier = pltpu.get_barrier_semaphore()
    for group, me, n in ((gs, me_s, n_seq), (gp, me_p, n_dp), (ge, me_e, n_ex)):
        for k in _issue_order(group, n):
            peer = _peer_coords(group, _offset_rank(group, n, me, k, 1))
            pl.semaphore_signal(barrier, inc=1, device_id=peer, device_id_type=MESH)

    logits = lax.dot_general(
        phi_ref[...], tok_v[...], (((1,), (1,)), ((), ())), preferred_element_type=jnp.float32
    )
    mx_ref[...] = jnp.broadcast_to(jnp.max(logits, axis=1, keepdims=True), mx_ref.shape)
    rows_out = lg_src.shape[2]
    for g in range(n_ex):
        lg_src[g] = logits[:, g * rows_out:(g + 1) * rows_out]
    pl.semaphore_wait(barrier, n_seq - 1 + n_dp - 1 + n_ex - 1)

    stage_a0 = (gs, me_s, n_seq, lambda c: mx_ref, mx_land, sems.at[14], sems.at[15])
    ex_pos = AXES.index("expert")
    stage_phi = (ge, me_e, n_ex, lambda c: lg_src.at[c[ex_pos]], lg_land, sems.at[4], sems.at[5])
    started_a0 = _send_all(*stage_a0)
    started_phi = _send_all(*stage_phi)
    _wait_all(*stage_a0, started_a0)
    mx_land[me_s] = mx_ref[...]
    slot_max = jnp.max(mx_land[...], axis=0)[:, 0:1]
    spread = jnp.exp(logits - slot_max)
    denominator = jnp.sum(spread, axis=1, keepdims=True)
    d = tok_v.shape[1]
    num_ref[:, 0:d] = jnp.dot(spread.astype(jnp.bfloat16), tok_v[...], preferred_element_type=jnp.float32)
    num_ref[:, d:d + 128] = jnp.broadcast_to(denominator, (denominator.shape[0], 128))

    stage_a = (gs, me_s, n_seq, lambda c: num_ref, num_land, sems.at[0], sems.at[1])
    _wait_all(*stage_a, _send_all(*stage_a))
    num_land[me_s] = num_ref[...]

    totals = jnp.sum(num_land[...], axis=0)
    si_src[...] = (totals[:, 0:d] / totals[:, d:d + 1]).astype(si_src.dtype)

    stage_a2 = (gp, me_p, n_dp, lambda c: si_src, si_land, sems.at[6], sems.at[7])
    _wait_all(*stage_a2, _send_all(*stage_a2))
    si_land[me_p] = si_src[...]
    own_e = num_ref.shape[0]
    for c in range(n_dp):
        value = si_land[c].astype(jnp.float32)
        for e in range(own_e):
            slot_in[e, pl.ds(c, 1), :] = value[e:e + 1, :]

    w_in_copy.wait()
    w_out_copy.wait()
    for e in range(own_e):
        hidden = jnp.dot(slot_in[e].astype(jnp.bfloat16), w_in_v[e], preferred_element_type=jnp.float32)
        hidden = _gelu(hidden).astype(jnp.bfloat16)
        part = jnp.dot(hidden, w_out_v[e], preferred_element_type=jnp.float32)
        for c in range(n_dp):
            part_src[c, pl.ds(e, 1), :] = part[c:c + 1, :]

    dp_pos = AXES.index("dp")
    stage_b1 = (gp, me_p, n_dp, lambda c: part_src.at[c[dp_pos]], pp_land, sems.at[8], sems.at[9])
    _wait_all(*stage_b1, _send_all(*stage_b1))
    partner = lax.rem(me_p + 1, n_dp)
    cs_src[...] = part_src[me_p] + pp_land[partner]

    stage_b2 = (gs, me_s, n_seq, lambda c: cs_src, cs_land, sems.at[10], sems.at[11])
    _wait_all(*stage_b2, _send_all(*stage_b2))
    cs_land[me_s] = cs_src[...]
    so_src[...] = jnp.sum(cs_land[...], axis=0).astype(so_src.dtype)

    stage_c = (ge, me_e, n_ex, lambda c: so_src, so_land, sems.at[12], sems.at[13])
    started_c = _send_all(*stage_c)
    _wait_all(*stage_phi, started_phi)
    lg_land[me_e] = lg_src[me_e]
    row_logits = lg_land[...]
    row_max = jnp.max(jnp.max(row_logits, axis=0), axis=0, keepdims=True)
    weights = jnp.exp(row_logits - row_max[None])
    wb_out[...] = weights.astype(wb_out.dtype)
    den_out[...] = jnp.sum(jnp.sum(weights, axis=0), axis=0, keepdims=True)
    _wait_all(*stage_c, started_c)
    so_land[me_e] = so_src[...]
    so_out[...] = so_land[...]


def expert_slots(tokens, phi_t, w_in, w_out, cid):
    n_dp, n_seq, n_ex = (lax.axis_size(a) for a in AXES)
    own_e, d = phi_t.shape
    vmem = pl.BlockSpec(memory_space=pltpu.VMEM)
    anywhere = pl.BlockSpec(memory_space=pl.ANY)
    gathered = jax.ShapeDtypeStruct((n_ex, own_e, d), jnp.bfloat16)
    rows_out = tokens.shape[0] // n_ex
    weights = jax.ShapeDtypeStruct((n_ex, own_e, rows_out), jnp.bfloat16)
    totals = jax.ShapeDtypeStruct((1, rows_out), jnp.float32)
    return pl.pallas_call(
        functools.partial(_slots_kernel, n_dp, n_seq, n_ex),
        out_shape=(weights, totals, gathered),
        in_specs=[vmem, vmem, anywhere, anywhere],
        out_specs=(vmem, vmem, vmem),
        scratch_shapes=[
            pltpu.VMEM((own_e, 128), jnp.float32),
            pltpu.VMEM((n_seq, own_e, 128), jnp.float32),
            pltpu.VMEM((own_e, d + 128), jnp.float32),
            pltpu.VMEM(w_in.shape, w_in.dtype),
            pltpu.VMEM(w_out.shape, w_out.dtype),
            pltpu.SemaphoreType.DMA((2,)),
            pltpu.VMEM((n_seq, own_e, d + 128), jnp.float32),
            pltpu.VMEM((n_ex, own_e, rows_out), jnp.float32),
            pltpu.VMEM((n_ex, own_e, rows_out), jnp.float32),
            pltpu.VMEM((own_e, d), jnp.bfloat16),
            pltpu.VMEM((n_dp, own_e, d), jnp.bfloat16),
            pltpu.VMEM((own_e, n_dp, d), jnp.float32),
            pltpu.VMEM((n_dp, own_e, d), jnp.float32),
            pltpu.VMEM((n_dp, own_e, d), jnp.float32),
            pltpu.VMEM((own_e, d), jnp.float32),
            pltpu.VMEM((n_seq, own_e, d), jnp.float32),
            pltpu.VMEM((own_e, d), jnp.bfloat16),
            pltpu.VMEM((n_ex, own_e, d), jnp.bfloat16),
            pltpu.SemaphoreType.DMA((16, max(n_dp, n_seq, n_ex))),
        ],
        compiler_params=pltpu.CompilerParams(
            collective_id=cid, has_side_effects=True, vmem_limit_bytes=48 * 1024 * 1024
        ),
    )(tokens, phi_t, w_in, w_out)

def on_device(tokens, phi, w_in, w_out):
    n_expert = lax.axis_size("expert")
    n_dp = lax.axis_size("dp")
    n_seq = lax.axis_size("seq")
    own_e = phi.shape[1]
    d = tokens.shape[1]
    rows_out = tokens.shape[0] // n_expert
    weight_g, total, slot_g = expert_slots(tokens, phi.T, w_in, w_out, 1)
    combine_weights = weight_g.reshape(n_expert * own_e, rows_out)
    slot_out = slot_g.reshape(n_expert * own_e, d)
    mixed_numer = lax.dot_general(
        combine_weights,
        slot_out,
        (((0,), (0,)), ((), ())),
        preferred_element_type=jnp.float32,
    )
    return (mixed_numer / total[0][:, None]).astype(jnp.bfloat16)


def solution(mesh):
    placed = (
        P(("dp", "seq"), None),
        P(None, "expert"),
        P("expert", None, ("dp", "seq")),
        P("expert", ("dp", "seq"), None),
    )
    return jax.shard_map(
        on_device,
        mesh=mesh,
        in_specs=placed,
        out_specs=P(("dp", "seq", "expert"), None),
        check_vma=False,
    )
```
